256 devices in a mesh: row: 8 (over x, z_lo), col: 32 (over y, z_hi, core).
Axes of the slice: x: 4, y: 4, z: 8 (z_hi: 4, z_lo: 2; z = z_hi * 2 + z_lo), core: 2. Of those that a mesh axis runs over, the one named last changes fastest.
Arguments:
- hamiltonian: float32 [4096, 4096], P('row', 'col'), as said below
- h_mask: int32 [32, 32], P('row', 'col'), may hold values from 0 to 1, as said below
- factor: float32 [4096, 4096], P('row', 'col'), may hold values from -0.125 to 0.125
- z_mask: int32 [32, 32], P('row', 'col'), may hold values 0 or 1
- k_mask: int32 [32, 32], P('row', 'col'), may hold values 0 or 1
- block_sizes: int32 [32], replicated, may hold values from 64 to 128, as said below
Outputs:
- transformed: float32 [4096, 4096], P('row', 'col')
The draws below stay inside these ranges and needn't reach their ends.
Inputs may be any that keep to these rules, and one draw needn't show every extreme that they name: hamiltonian is symmetric. `h_mask`: symmetric, with every diagonal block occupied. `block_sizes`: some block uses all 128 orbitals.
All inputs are finite; a program needn't handle non-finite values. No bound on the sum of `z_mask` or of `k_mask` on one device may be relied on, other than what follows from the above.
Results may differ from the reference program's by a relative error of at most 0.000098.
Values sent between devices are 32-bit elements; how exact they have to be, the bound alone decides.
A program may use at most 64 MiB of HBM per device.

```python
import jax
import jax.numpy as jnp
from jax import lax

BLOCK = 128
NBLK = 32
ORDER = 4096


def draw_hamiltonian(key, part):
    count = NBLK * BLOCK
    base = jax.random.normal(key, (count, count), jnp.float32)
    return (base + base.T) * 0.7071


def draw_h_mask(key, part):
    picks = jax.random.randint(key, (NBLK, NBLK), 0, 4)
    ones = (picks < 3).astype(jnp.int32)
    both = ones * ones.T
    eye = jnp.eye(NBLK, dtype=jnp.int32)
    return jnp.maximum(both, eye)


def draw_block_sizes(key, part):
    values = jax.random.randint(key, (NBLK,), BLOCK // 2, BLOCK + 1)
    spot = jax.random.randint(jax.random.fold_in(key, 3), (), 0, NBLK)
    return jnp.where(jnp.arange(NBLK) == spot, BLOCK, values).astype(jnp.int32)


def plant(array, key, least, top_value):
    extent = array.shape
    spot = [jax.random.randint(jax.random.fold_in(key, axis), (), 0, extent[axis]) for axis in range(len(extent))]
    array = array.at[tuple(spot)].set(least)
    longest = extent.index(max(extent))
    spot[longest] = (spot[longest] + 1) % extent[longest]
    return array.at[tuple(spot)].set(top_value)


def block_levels(own_key, shape, cuts, low, top_value):
    loudness, own = 1.0, jax.random.fold_in(own_key, 6)
    for axis_at, parts in cuts:
        draws = jnp.exp(jax.random.uniform(jax.random.fold_in(own, axis_at), (parts,), jnp.float32, low / len(cuts), top_value / len(cuts)))
        loudness = loudness * jnp.repeat(draws, shape[axis_at] // parts).reshape([-1 if axis == axis_at else 1 for axis in range(len(shape))])
    return loudness


def normal_values(stream_key, shape, deviation, bound, cuts=(), kind=jnp.bfloat16):
    drawn = deviation * jax.random.normal(stream_key, shape, jnp.float32)
    if cuts:
        drawn = drawn * block_levels(stream_key, shape, cuts, -0.22, 0.18)
    return jnp.clip(drawn, -bound, bound).astype(kind)


def setup_inputs(seed: int = 0) -> dict:
    arg_keys = jax.random.split(jax.random.key(seed), 7)
    return {
        "hamiltonian": draw_hamiltonian(jax.random.fold_in(arg_keys[6], 71), 0),
        "h_mask": draw_h_mask(jax.random.fold_in(arg_keys[6], 71), 0),
        "factor": normal_values(arg_keys[2], (ORDER, ORDER), (ORDER // 2) ** -0.5, 0.125, ((0, 8), (1, 32)), jnp.float32),
        "z_mask": plant((jax.random.randint(arg_keys[3], (NBLK, NBLK), 0, 4) < 3).astype(jnp.int32), jax.random.fold_in(arg_keys[3], 1), 0, 1),
        "k_mask": plant((jax.random.randint(arg_keys[4], (NBLK, NBLK), 0, 4) < 3).astype(jnp.int32), jax.random.fold_in(arg_keys[4], 1), 0, 1),
        "block_sizes": draw_block_sizes(jax.random.fold_in(arg_keys[6], 71), 0),
    }


def expand(blocks):
    grown = jnp.repeat(blocks.astype(jnp.float32), BLOCK, axis=0)
    return jnp.repeat(grown, BLOCK, axis=1)


def reference(hamiltonian, h_mask, factor, z_mask, k_mask, block_sizes):
    index = jnp.arange(ORDER, dtype=jnp.int32)
    limits = jnp.repeat(block_sizes, BLOCK)
    valid = (index % BLOCK < limits).astype(jnp.float32)
    outer = valid[:, None] * valid[None, :]
    hmat = hamiltonian * expand(h_mask) * outer
    upper = (index[:, None] <= index[None, :]).astype(jnp.float32)
    zmat = factor * expand(z_mask) * outer * upper
    hz = jnp.dot(hmat, zmat, precision=lax.Precision.HIGHEST, preferred_element_type=jnp.float32)
    result = jnp.dot(zmat.T, hz, precision=lax.Precision.HIGHEST, preferred_element_type=jnp.float32)
    return result * expand(k_mask)
```

```python
import jax
import jax.numpy as jnp
from jax import lax
from jax.experimental import pallas as pl
from jax.experimental.pallas import tpu as pltpu
from jax.sharding import PartitionSpec as P

B = 128
MESH = pl.DeviceIdType.MESH
ORDER = (0, 2, 1, 3)
F32 = jnp.float32


def split(v):
    hi = v.astype(jnp.bfloat16)
    return hi, (v - hi.astype(F32)).astype(jnp.bfloat16)


def dot(a, b):
    return jnp.dot(a, b, preferred_element_type=F32)


def dot3(ah, al, bh, bl):
    return dot(ah, bh) + (dot(ah, bl) + dot(al, bh))


def kernel(h_ref, hm_ref, z_ref, zm_ref, km_ref, size_ref, out_ref,
           hg, zg, sw, xg, z1, z1h, z1l, wp, cr, wc, yr, wt, wh, wl, u, xr, fin, tr,
           h_ss, h_rs, z_ss, z_rs, sw_s, ce_s, xa_ss, xa_rs, ya_ss, ya_rs,
           wc_ss, wc_rs, wy_ss, wy_rs, wa_ss, wa_rs, wf_ss, wf_rs, ux_ss, ux_rs, fd_ss, fd_rs):
    row = lax.axis_index("row")
    col = lax.axis_index("col")
    x, zl = row // 2, row % 2
    y, zh, c = col // 8, (col // 2) % 4, col % 2
    z = zh * 2 + zl

    def dev(x_, y_, z_, c_):
        return (x_ * 2 + z_ % 2, (y_ * 4 + z_ // 2) * 2 + c_)

    def remote(src, dst, ss, rs, to):
        return pltpu.make_async_remote_copy(
            src_ref=src, dst_ref=dst, send_sem=ss, recv_sem=rs, device_id=to, device_id_type=MESH)

    sib = dev(x, y, z, 1 - c)
    xpeer = [None] + [dev((x + d) % 4, y, z, c) for d in (1, 2, 3)]
    ypeer = [None] + [dev(x, (y + d) % 4, z, c) for d in (1, 2, 3)]
    zpeer = [dev(x, y, (z + 1) % 8, c), dev(x, y, (z + 7) % 8, c)]
    partner = dev(x, y, zh * 2 + c, zl)
    crossed = zl != c
    homed = zl == zh // 2

    barrier = pltpu.get_barrier_semaphore()
    for to in [sib] + xpeer[1:] + ypeer[1:] + zpeer:
        pl.semaphore_signal(barrier, inc=1, device_id=to, device_id_type=MESH)

    @pl.when(crossed)
    def _():
        pl.semaphore_signal(barrier, inc=1, device_id=partner, device_id_type=MESH)

    for b in range(4):
        @pl.when(zl * 4 + b != z)
        def _():
            pl.semaphore_signal(barrier, inc=1, device_id=dev(x, y, zl * 4 + b, c), device_id_type=MESH)

    ri = lax.broadcasted_iota(jnp.int32, (B, B), 0)
    ci = lax.broadcasted_iota(jnp.int32, (B, B), 1)
    colok = ci < size_ref[col]
    for s, b in enumerate(ORDER):
        rb = row * 4 + b
        ok = jnp.logical_and(colok, ri < size_ref[rb]).astype(F32)
        hg[z, s * B:(s + 1) * B, :] = h_ref[b * B:(b + 1) * B, :] * (ok * hm_ref[b, 0].astype(F32))
        up = (ri + rb * B <= ci + col * B).astype(F32)
        zg[z, s * B:(s + 1) * B, :] = z_ref[b * B:(b + 1) * B, :] * (ok * up * zm_ref[b, 0].astype(F32))

    pl.semaphore_wait(barrier, 13 + crossed.astype(jnp.int32) - homed.astype(jnp.int32))

    def ring(buf, ss, rs):
        made = {}

        def step(st, subs):
            for s in subs:
                for d in range(2):
                    if st > 0:
                        made[st - 1, s, d].wait_recv()
                    if st == 3 and s % 2 != d:
                        continue
                    slot = (z + 8 - st) % 8 if d == 0 else (z + st) % 8
                    part = buf.at[slot, pl.ds(s * B, B)]
                    cp = remote(part, part, ss.at[d, st, s], rs.at[d, st, s], zpeer[d])
                    cp.start()
                    made[st, s, d] = cp

        def last(subs):
            for s in subs:
                made[3, s, s % 2].wait_recv()

        def sent():
            for cp in made.values():
                cp.wait_send()

        return step, last, sent

    hstep, hlast, hsent = ring(hg, h_ss, h_rs)
    zstep, zlast, zsent = ring(zg, z_ss, z_rs)

    hstep(0, (0, 1))

    swap = remote(zg.at[z], sw, sw_s.at[0], sw_s.at[1], partner)

    @pl.when(crossed)
    def _():
        swap.start()

    @pl.when(jnp.logical_not(crossed))
    def _():
        sw[...] = zg[z]

    @pl.when(crossed)
    def _():
        swap.wait_recv()

    mine = pl.ds(pl.multiple_of(c * 256, 256), 256)
    other = pl.ds(pl.multiple_of((1 - c) * 256, 256), 256)
    cex = remote(sw.at[other], xg.at[x, mine], ce_s.at[0], ce_s.at[1], sib)
    cex.start()
    xg[x, mine, :] = sw[mine, :]
    hstep(1, (0, 1))
    cex.wait_recv()
    xa = {}
    for d in (1, 3, 2):
        xa[d] = remote(xg.at[x], xg.at[x], xa_ss.at[d], xa_rs.at[d], xpeer[d])
        xa[d].start()
    ya = {}

    def ysend(e):
        src = (x + 4 - e) % 4
        d = (src + 4 - y) % 4
        ya[e] = d, remote(xg.at[src], z1.at[y], ya_ss.at[e], ya_rs.at[d], dev(x, src, z, c))

        @pl.when(d != 0)
        def _():
            ya[e][1].start()

    ysend(0)
    hstep(2, (0, 1))
    for e in (1, 3):
        xa[e].wait_recv()
        ysend(e)
    hstep(3, (0, 1))
    hstep(0, (2, 3))
    xa[2].wait_recv()
    ysend(2)
    z1[y] = xg[y]
    hlast((0, 1))
    hstep(1, (2, 3))
    for d in (1, 2, 3):
        remote(xg.at[0], z1.at[y], ya_ss.at[0], ya_rs.at[d], sib).wait_recv()
    for j in range(4):
        hi, lo = split(z1[j])
        z1h[:, j * B:(j + 1) * B] = hi
        z1l[:, j * B:(j + 1) * B] = lo

    def first(k):
        rows = slice(k * 256, (k + 1) * 256)
        for half in range(2):
            a = jnp.concatenate([hg[2 * q + half, rows, :] for q in range(4)], axis=1)
            ah, al = split(a)
            wp[k, half * 256:(half + 1) * 256, :] = dot3(ah, al, z1h[...], z1l[...])
        cp = remote(wp.at[k, other], cr.at[k], wc_ss.at[k], wc_rs.at[k], sib)
        cp.start()
        return cp

    def scatter(k, cp):
        cp.wait_recv()
        tot = wp[k, mine, :] + cr[k]
        for q in range(4):
            wc[k, q] = tot[:, q * B:(q + 1) * B]
        cps = {}
        for d in (1, 3, 2):
            cps[d] = remote(wc.at[k, (y + d) % 4], yr.at[k, d - 1], wy_ss.at[k, d], wy_rs.at[k, d], ypeer[d])
            cps[d].start()
        return cps

    def spread(k, cps):
        for d in (1, 3, 2):
            cps[d].wait_recv()
        r = (wc[k, y] + yr[k, 0]) + (yr[k, 1] + yr[k, 2])
        wt[k, y, c] = r.T
        own = wt.at[k, y, c]
        out = {}
        for d in (1, 3, 2):
            out[d] = remote(own, own, wa_ss.at[k, d], wa_rs.at[k, d], ypeer[d])
            out[d].start()
        out[0] = remote(own, own, wf_ss.at[k, 0], wf_rs.at[k, 0], sib)
        out[0].start()
        return out

    def forward(k, out):
        fw = {}
        for d in (1, 3, 2):
            out[d].wait_recv()
            part = wt.at[k, (y + 4 - d) % 4, c]
            fw[d] = remote(part, part, wf_ss.at[k, d], wf_rs.at[k, d], sib)
            fw[d].start()
        return fw

    def gathered(k, out, fw):
        out[0].wait_recv()
        for d in (1, 3, 2):
            fw[d].wait_recv()
        for q in range(4):
            for half in range(2):
                hi, lo = split(wt[k, q, half])
                at = (k * 2 + half) * 256
                wh[q * B:(q + 1) * B, at:at + 256] = hi
                wl[q * B:(q + 1) * B, at:at + 256] = lo

    c0 = first(0)
    hstep(2, (2, 3))
    s0 = scatter(0, c0)
    hstep(3, (2, 3))
    zstep(0, (0, 1, 2, 3))
    o0 = spread(0, s0)
    hlast((2, 3))
    c1 = first(1)
    f0 = forward(0, o0)
    s1 = scatter(1, c1)
    zstep(1, (0, 1, 2, 3))
    gathered(0, o0, f0)
    o1 = spread(1, s1)
    f1 = forward(1, o1)
    gathered(1, o1, f1)

    shift = zl * 2 + 3
    near = [zh, (zh + shift) % 4, (zh + 4 - shift % 4) % 4, (zh + 2) % 4]

    def second(j):
        zz = near[j]
        b = jnp.concatenate(
            [zg[zz * 2 + half, k * 256:(k + 1) * 256, :] for k in range(2) for half in range(2)], axis=0)
        bh, bl = split(b)
        t = dot3(wh[...], wl[...], bh, bl)
        for q in range(4):
            u[j, q] = t[q * B:(q + 1) * B, :]
        cps = {}
        for d in (1, 3, 2):
            cps[d] = remote(u.at[j, (x + d) % 4], xr.at[j, d - 1], ux_ss.at[j, d], ux_rs.at[j, d], xpeer[d])
            cps[d].start()
        return cps

    place = (zh % 2) * 2 + zl
    away = [None] * 4

    def deliver(j, cps):
        for d in (1, 3, 2):
            cps[d].wait_recv()
        v = (u[j, x] + xr[j, 0]) + (xr[j, 1] + xr[j, 2])
        fin[j] = v
        away[j] = remote(fin.at[j], tr.at[place], fd_ss.at[j], fd_rs.at[place],
                         dev(x, y, near[j] * 2 + zh // 2, c))
        if j == 0:
            @pl.when(homed)
            def _():
                tr[place] = fin[0]

            @pl.when(jnp.logical_not(homed))
            def _():
                away[0].start()
        else:
            away[j].start()

    u0 = second(0)
    zstep(2, (0, 1, 2, 3))
    u1 = second(1)
    deliver(0, u0)
    zstep(3, (0, 1, 2, 3))
    u2 = second(2)
    deliver(1, u1)
    zlast((0, 1, 2, 3))
    u3 = second(3)
    deliver(2, u2)
    deliver(3, u3)
    for b in range(4):
        @pl.when(zl * 4 + b != z)
        def _():
            remote(fin.at[0], tr.at[b], fd_ss.at[0], fd_rs.at[b], sib).wait_recv()

        out_ref[b * B:(b + 1) * B, :] = tr[b] * km_ref[b, 0].astype(F32)

    hsent()
    zsent()

    @pl.when(crossed)
    def _():
        swap.wait_send()

    cex.wait_send()
    for d in (1, 2, 3):
        xa[d].wait_send()
    for e in range(4):
        @pl.when(ya[e][0] != 0)
        def _():
            ya[e][1].wait_send()
    for group in (s0, s1, o0, o1, f0, f1, u0, u1, u2, u3):
        for cp in group.values():
            cp.wait_send()
    c0.wait_send()
    c1.wait_send()

    @pl.when(jnp.logical_not(homed))
    def _():
        away[0].wait_send()

    for j in (1, 2, 3):
        away[j].wait_send()


def local(hamiltonian, h_mask, factor, z_mask, k_mask, block_sizes):
    vm = pl.BlockSpec(memory_space=pltpu.VMEM)
    sm = pl.BlockSpec(memory_space=pltpu.SMEM)
    dma = pltpu.SemaphoreType.DMA
    bf = jnp.bfloat16
    scratch = [
        pltpu.VMEM((8, 512, B), F32),
        pltpu.VMEM((8, 512, B), F32),
        pltpu.VMEM((512, B), F32),
        pltpu.VMEM((4, 512, B), F32),
        pltpu.VMEM((4, 512, B), F32),
        pltpu.VMEM((512, 512), bf),
        pltpu.VMEM((512, 512), bf),
        pltpu.VMEM((2, 512, 512), F32),
        pltpu.VMEM((2, 256, 512), F32),
        pltpu.VMEM((2, 4, 256, B), F32),
        pltpu.VMEM((2, 3, 256, B), F32),
        pltpu.VMEM((2, 4, 2, B, 256), F32),
        pltpu.VMEM((512, 1024), bf),
        pltpu.VMEM((512, 1024), bf),
        pltpu.VMEM((4, 4, B, B), F32),
        pltpu.VMEM((4, 3, B, B), F32),
        pltpu.VMEM((4, B, B), F32),
        pltpu.VMEM((4, B, B), F32),
        dma((2, 4, 4)), dma((2, 4, 4)), dma((2, 4, 4)), dma((2, 4, 4)),
        dma((2,)), dma((2,)), dma((4,)), dma((4,)), dma((4,)), dma((4,)),
        dma((2,)), dma((2,)), dma((2, 4)), dma((2, 4)), dma((2, 4)), dma((2, 4)),
        dma((2, 4)), dma((2, 4)), dma((4, 4)), dma((4, 4)), dma((4,)), dma((4,)),
    ]
    return pl.pallas_call(
        kernel,
        out_shape=jax.ShapeDtypeStruct((512, B), F32),
        in_specs=[vm, sm, vm, sm, sm, sm],
        out_specs=vm,
        scratch_shapes=scratch,
        compiler_params=pltpu.CompilerParams(
            collective_id=0, has_side_effects=True, vmem_limit_bytes=48 << 20),
        name="congruence",
    )(hamiltonian, h_mask, factor, z_mask, k_mask, block_sizes)


def solution(mesh):
    placed = (
        P("row", "col"),
        P("row", "col"),
        P("row", "col"),
        P("row", "col"),
        P("row", "col"),
        P(),
    )
    return jax.shard_map(
        local, mesh=mesh, in_specs=placed, out_specs=P("row", "col"), check_vma=False
    )
```

```python
import jax
import jax.numpy as jnp
from jax import lax
from jax.experimental import pallas as pl
from jax.experimental.pallas import tpu as pltpu
from jax.sharding import PartitionSpec as P

B = 128
MESH = pl.DeviceIdType.MESH
ORDER = (0, 2, 1, 3)
F32 = jnp.float32
CHUNKS = 2
HALF = B // CHUNKS


def split(v):
    hi = v.astype(jnp.bfloat16)
    return hi, (v - hi.astype(F32)).astype(jnp.bfloat16)


def dot3(ah, al, bh, bl):
    return jnp.dot(jnp.concatenate([ah, ah, al], axis=1), jnp.concatenate([bh, bl, bh], axis=0),
                   preferred_element_type=F32)


def kernel(h_hbm, hm_hbm, z_hbm, zm_hbm, km_hbm, size_hbm, out_ref,
           h_ref, z_ref, hm_ref, zm_ref, km_ref, size_ref, in_s,
           hg, zg, ah, al, bh, bl, sw, xg, z1, z1h, z1l, wp, cr, wc, yr, wt, u, xr, fin, tr,
           h_ss, h_rs, z_ss, z_rs, sw_s, ce_s, xa_ss, xa_rs, ya_ss, ya_rs,
           wc_ss, wc_rs, wy_ss, wy_rs, wa_ss, wa_rs, wf_ss, wf_rs, ux_ss, ux_rs, fd_ss, fd_rs):
    row = lax.axis_index("row")
    col = lax.axis_index("col")
    x, zl = row // 2, row % 2
    y, zh, c = col // 8, (col // 2) % 4, col % 2
    z = zh * 2 + zl

    loads = [
        pltpu.make_async_copy(src, dst, in_s.at[i])
        for i, (src, dst) in enumerate([
            (size_hbm, size_ref), (zm_hbm, zm_ref), (z_hbm, z_ref), (hm_hbm, hm_ref), (h_hbm, h_ref), (km_hbm, km_ref)])
    ]
    for cp in loads:
        cp.start()

    def dev(x_, y_, z_, c_):
        return (x_ * 2 + z_ % 2, (y_ * 4 + z_ // 2) * 2 + c_)

    def remote(src, dst, ss, rs, to):
        return pltpu.make_async_remote_copy(
            src_ref=src, dst_ref=dst, send_sem=ss, recv_sem=rs, device_id=to, device_id_type=MESH)

    sib = dev(x, y, z, 1 - c)
    xpeer = [None] + [dev((x + d) % 4, y, z, c) for d in (1, 2, 3)]
    ypeer = [None] + [dev(x, (y + d) % 4, z, c) for d in (1, 2, 3)]
    zpeer = [dev(x, y, (z + 1) % 8, c), dev(x, y, (z + 7) % 8, c)]
    partner = dev(x, y, zh * 2 + c, zl)
    crossed = zl != c
    homed = zl == zh // 2

    barrier = pltpu.get_barrier_semaphore()
    for to in [sib] + xpeer[1:] + ypeer[1:] + zpeer:
        pl.semaphore_signal(barrier, inc=1, device_id=to, device_id_type=MESH)

    @pl.when(crossed)
    def _():
        pl.semaphore_signal(barrier, inc=1, device_id=partner, device_id_type=MESH)

    for b in range(4):
        @pl.when(zl * 4 + b != z)
        def _():
            pl.semaphore_signal(barrier, inc=1, device_id=dev(x, y, zl * 4 + b, c), device_id_type=MESH)

    for cp in loads:
        cp.wait()
    ri = lax.broadcasted_iota(jnp.int32, (B, B), 0)
    ci = lax.broadcasted_iota(jnp.int32, (B, B), 1)
    colok = ci < size_ref[col]
    for s, b in enumerate(ORDER):
        rb = row * 4 + b
        ok = jnp.logical_and(colok, ri < size_ref[rb]).astype(F32)
        up = (ri + rb * B <= ci + col * B).astype(F32)
        zg[z, s * B:(s + 1) * B, :] = z_ref[b * B:(b + 1) * B, :] * (ok * up * zm_ref[0, b].astype(F32))
        hg[z, s * B:(s + 1) * B, :] = h_ref[b * B:(b + 1) * B, :] * (ok * hm_ref[0, b].astype(F32))

    pl.semaphore_wait(barrier, 13 + crossed.astype(jnp.int32) - homed.astype(jnp.int32))

    swap = remote(zg.at[z], sw, sw_s.at[0], sw_s.at[1], partner)

    @pl.when(crossed)
    def _():
        swap.start()

    @pl.when(jnp.logical_not(crossed))
    def _():
        sw[...] = zg[z]

    def ring(buf, ss, rs):
        made = {}

        def step(st, s):
            for d in range(2):
                if st > 0:
                    made[st - 1, s, d].wait_recv()
                if st == 3 and s % 2 != d:
                    continue
                slot = (z + 8 - st) % 8 if d == 0 else (z + st) % 8
                part = buf.at[slot, pl.ds(s * B, B)]
                cp = remote(part, part, ss.at[d, st, s], rs.at[d, st, s], zpeer[d])
                cp.start()
                made[st, s, d] = cp

        def last():
            for s in range(4):
                made[3, s, s % 2].wait_recv()

        def sent():
            for cp in made.values():
                cp.wait_send()

        return step, last, sent

    hstep, hlast, hsent = ring(hg, h_ss, h_rs)
    zstep, zlast, zsent = ring(zg, z_ss, z_rs)

    def parts(buf, hi_ref, lo_ref, dist):
        for slot in {0: [z], 4: [(z + 4) % 8]}.get(dist, [(z + dist) % 8, (z + 8 - dist) % 8]):
            hi, lo = split(buf[slot])
            hi_ref[slot] = hi
            lo_ref[slot] = lo

    for s in range(4):
        hstep(0, s)
    parts(hg, ah, al, 0)

    @pl.when(crossed)
    def _():
        swap.wait_recv()

    mine = pl.ds(pl.multiple_of(c * 256, 256), 256)
    other = pl.ds(pl.multiple_of((1 - c) * 256, 256), 256)
    cex = remote(sw.at[other], xg.at[x, mine], ce_s.at[0], ce_s.at[1], sib)
    cex.start()
    xg[x, mine, :] = sw[mine, :]
    hstep(1, 0)
    cex.wait_recv()
    xa = {}
    for d in (1, 3, 2):
        xa[d] = remote(xg.at[x], xg.at[x], xa_ss.at[d], xa_rs.at[d], xpeer[d])
        xa[d].start()
    ya = {}

    def ysend(e):
        src = (x + 4 - e) % 4
        d = (src + 4 - y) % 4
        ya[e] = d, remote(xg.at[src], z1.at[y], ya_ss.at[e], ya_rs.at[d], dev(x, src, z, c))

        @pl.when(d != 0)
        def _():
            ya[e][1].start()

    ysend(0)
    hstep(1, 1)
    hstep(1, 2)
    hstep(1, 3)
    parts(hg, ah, al, 1)
    hstep(2, 0)
    for e in (1, 3):
        xa[e].wait_recv()
        ysend(e)
    hstep(2, 1)
    hstep(2, 2)
    xa[2].wait_recv()
    ysend(2)
    z1[y] = xg[y]
    hstep(2, 3)
    parts(hg, ah, al, 2)
    for s in range(4):
        hstep(3, s)
    for s in range(4):
        zstep(0, s)
    parts(hg, ah, al, 3)
    parts(zg, bh, bl, 0)
    for d in (1, 2, 3):
        remote(xg.at[0], z1.at[y], ya_ss.at[0], ya_rs.at[d], sib).wait_recv()
    left = lax.broadcasted_iota(jnp.int32, (512, B), 1) < HALF
    for p in range(2):
        v0, v1 = z1[2 * p], z1[2 * p + 1]
        for m, v in enumerate([jnp.where(left, v0, pltpu.roll(v1, HALF, 1)),
                               jnp.where(left, pltpu.roll(v0, HALF, 1), v1)]):
            hi, lo = split(v)
            z1h[m, :, p * B:(p + 1) * B] = hi
            z1l[m, :, p * B:(p + 1) * B] = lo
    hlast()
    parts(hg, ah, al, 4)

    def whole(ref):
        return jnp.concatenate(
            [jnp.concatenate([ref[2 * q + half] for q in range(4)], axis=1) for half in range(2)], axis=0)

    crow = pl.ds(pl.multiple_of(c * 512, 512), 512)
    orow = pl.ds(pl.multiple_of((1 - c) * 512, 512), 512)

    def first(m):
        wp[m] = dot3(whole(ah), whole(al), z1h[m], z1l[m])
        cp = remote(wp.at[m, orow], cr.at[m], wc_ss.at[m], wc_rs.at[m], sib)
        cp.start()
        return cp

    def scatter(m, cp):
        cp.wait_recv()
        wc[m] = wp[m, crow, :] + cr[m]
        cps = {}
        for d in (1, 3, 2):
            piece = pl.ds(pl.multiple_of(((y + d) % 4) * B, B), B)
            cps[d] = remote(wc.at[m, piece], yr.at[m, d - 1], wy_ss.at[m, d], wy_rs.at[m, d], ypeer[d])
            cps[d].start()
        return cps

    def spread(m, cps):
        for d in (1, 3, 2):
            cps[d].wait_recv()
        r = (wc[m, pl.ds(pl.multiple_of(y * B, B), B), :] + yr[m, 0]) + (yr[m, 1] + yr[m, 2])
        wt[m, c, y] = r.T
        own = wt.at[m, c, y]
        out = {}
        for d in (1, 3, 2):
            out[d] = remote(own, own, wa_ss.at[m, d], wa_rs.at[m, d], ypeer[d])
            out[d].start()
        out[0] = remote(own, own, wf_ss.at[m, 0], wf_rs.at[m, 0], sib)
        out[0].start()
        return out

    def forward(m, out):
        fw = {}
        for d in (1, 3, 2):
            out[d].wait_recv()
            part = wt.at[m, c, (y + 4 - d) % 4]
            fw[d] = remote(part, part, wf_ss.at[m, d], wf_rs.at[m, d], sib)
            fw[d].start()
        return fw

    c0 = first(0)
    c1 = first(1)
    s0 = scatter(0, c0)
    zstep(1, 0)
    zstep(1, 1)
    s1 = scatter(1, c1)
    zstep(1, 2)
    zstep(1, 3)
    parts(zg, bh, bl, 1)
    o0 = spread(0, s0)
    for s in range(4):
        zstep(2, s)
    parts(zg, bh, bl, 2)
    o1 = spread(1, s1)
    for s in range(4):
        zstep(3, s)
    f0 = forward(0, o0)
    parts(zg, bh, bl, 3)
    zlast()
    parts(zg, bh, bl, 4)

    def second(m, out, fw):
        out[0].wait_recv()
        for d in (1, 3, 2):
            fw[d].wait_recv()
        a = jnp.concatenate([wt[m, half, s] for half in range(2) for s in range(4)], axis=1)
        hi, lo = split(a)
        t = dot3(hi, lo, whole(bh), whole(bl))
        for q in range(4):
            u[m, q] = t[q * HALF:(q + 1) * HALF, :]
        cps = {}
        for d in (1, 3, 2):
            cps[d] = remote(u.at[m, (x + d) % 4], xr.at[m, d - 1], ux_ss.at[m, d], ux_rs.at[m, d], xpeer[d])
            cps[d].start()
        return cps

    place = (zh % 2) * 2 + zl
    away = {}

    def deliver(m, cps):
        for d in (1, 3, 2):
            cps[d].wait_recv()
        v = (u[m, x] + xr[m, 0]) + (xr[m, 1] + xr[m, 2])
        for q in range(4):
            fin[m, q] = v[:, q * B:(q + 1) * B]
            to = 2 * q + zh // 2
            cp = remote(fin.at[m, q], tr.at[place, m], fd_ss.at[m, q], fd_rs.at[m, place], dev(x, y, to, c))
            away[m, q] = to, cp

            @pl.when(to == z)
            def _():
                tr[place, m] = fin[m, q]

            @pl.when(to != z)
            def _():
                cp.start()

    u0 = second(0, o0, f0)
    f1 = forward(1, o1)
    u1 = second(1, o1, f1)
    deliver(0, u0)
    deliver(1, u1)
    for m in range(CHUNKS):
        for b in range(4):
            @pl.when(zl * 4 + b != z)
            def _():
                remote(fin.at[0, 0], tr.at[b, m], fd_ss.at[0, 0], fd_rs.at[m, b], sib).wait_recv()

            out_ref[b * B + m * HALF:b * B + (m + 1) * HALF, :] = tr[b, m] * km_ref[0, b].astype(F32)

    hsent()
    zsent()

    @pl.when(crossed)
    def _():
        swap.wait_send()

    cex.wait_send()
    for d in (1, 2, 3):
        xa[d].wait_send()
    for e in range(4):
        @pl.when(ya[e][0] != 0)
        def _():
            ya[e][1].wait_send()
    for group in (s0, s1, o0, o1, f0, f1, u0, u1):
        for cp in group.values():
            cp.wait_send()
    c0.wait_send()
    c1.wait_send()
    for to, cp in away.values():
        @pl.when(to != z)
        def _():
            cp.wait_send()


def local(hamiltonian, h_mask, factor, z_mask, k_mask, block_sizes):
    dma = pltpu.SemaphoreType.DMA
    bf = jnp.bfloat16
    flags = pltpu.SMEM((1, 4), jnp.int32)
    scratch = [
        pltpu.VMEM((512, B), F32), pltpu.VMEM((512, B), F32), flags, flags, flags,
        pltpu.SMEM((32,), jnp.int32), dma((6,)),
        pltpu.VMEM((8, 512, B), F32),
        pltpu.VMEM((8, 512, B), F32),
        pltpu.VMEM((8, 512, B), bf), pltpu.VMEM((8, 512, B), bf),
        pltpu.VMEM((8, 512, B), bf), pltpu.VMEM((8, 512, B), bf),
        pltpu.VMEM((512, B), F32),
        pltpu.VMEM((4, 512, B), F32),
        pltpu.VMEM((4, 512, B), F32),
        pltpu.VMEM((CHUNKS, 512, 256), bf), pltpu.VMEM((CHUNKS, 512, 256), bf),
        pltpu.VMEM((CHUNKS, 1024, 256), F32),
        pltpu.VMEM((CHUNKS, 512, 256), F32),
        pltpu.VMEM((CHUNKS, 512, 256), F32),
        pltpu.VMEM((CHUNKS, 3, B, 256), F32),
        pltpu.VMEM((CHUNKS, 2, 4, 256, B), F32),
        pltpu.VMEM((CHUNKS, 4, HALF, 512), F32),
        pltpu.VMEM((CHUNKS, 3, HALF, 512), F32),
        pltpu.VMEM((CHUNKS, 4, HALF, B), F32),
        pltpu.VMEM((4, CHUNKS, HALF, B), F32),
        dma((2, 4, 4)), dma((2, 4, 4)), dma((2, 4, 4)), dma((2, 4, 4)),
        dma((2,)), dma((2,)), dma((4,)), dma((4,)), dma((4,)), dma((4,)),
        dma((2,)), dma((2,)), dma((2, 4)), dma((2, 4)), dma((2, 4)), dma((2, 4)),
        dma((2, 4)), dma((2, 4)), dma((2, 4)), dma((2, 4)), dma((2, 4)), dma((2, 4)),
    ]
    hbm = pl.BlockSpec(memory_space=pltpu.HBM)
    return pl.pallas_call(
        kernel,
        out_shape=jax.ShapeDtypeStruct((512, B), F32),
        in_specs=[hbm] * 6,
        out_specs=pl.BlockSpec(memory_space=pltpu.VMEM),
        scratch_shapes=scratch,
        compiler_params=pltpu.CompilerParams(
            collective_id=0, has_side_effects=True, vmem_limit_bytes=64 << 20),
        name="congruence",
    )(hamiltonian, h_mask.reshape(1, 4), factor, z_mask.reshape(1, 4), k_mask.reshape(1, 4), block_sizes)


def solution(mesh):
    placed = (
        P("row", "col"),
        P("row", "col"),
        P("row", "col"),
        P("row", "col"),
        P("row", "col"),
        P(),
    )
    return jax.shard_map(
        local, mesh=mesh, in_specs=placed, out_specs=P("row", "col"), check_vma=False
    )
```

```python
import jax
import jax.numpy as jnp
from jax import lax
from jax.experimental import pallas as pl
from jax.experimental.pallas import tpu as pltpu
from jax.sharding import PartitionSpec as P

B = 128
MESH = pl.DeviceIdType.MESH
ORDER = (0, 2, 1, 3)
F32 = jnp.float32
CHUNKS = 2
HALF = B // CHUNKS


def split(v):
    hi = v.astype(jnp.bfloat16)
    return hi, (v - hi.astype(F32)).astype(jnp.bfloat16)


def dot3(ah, al, bh, bl, axis):
    return lax.dot_general(
        jnp.concatenate([ah, ah, al], axis=1), jnp.concatenate([bh, bl, bh], axis=axis),
        (((1,), (axis,)), ((), ())), preferred_element_type=F32)


def kernel(h_hbm, hm_hbm, z_hbm, zm_hbm, km_hbm, size_hbm, out_ref,
           h_ref, z_ref, hm_ref, zm_ref, km_ref, size_ref, in_s,
           hg, zg, ah, al, bh, bl, sw, z1, z1h, z1l, wp, cr, wc, yr, wt, u, xr, fin, tr,
           h_ss, h_rs, z_ss, z_rs, sw_s, z1_ss, z1_rs,
           wc_ss, wc_rs, wy_ss, wy_rs, wa_ss, wa_rs, wf_ss, wf_rs, ux_ss, ux_rs, fd_ss, fd_rs):
    row = lax.axis_index("row")
    col = lax.axis_index("col")
    x, zl = row // 2, row % 2
    y, zh, c = col // 8, (col // 2) % 4, col % 2
    z = zh * 2 + zl

    loads = [
        pltpu.make_async_copy(src, dst, in_s.at[i])
        for i, (src, dst) in enumerate([
            (size_hbm, size_ref), (zm_hbm, zm_ref), (z_hbm, z_ref), (hm_hbm, hm_ref), (h_hbm, h_ref), (km_hbm, km_ref)])
    ]
    for cp in loads:
        cp.start()

    def dev(x_, y_, z_, c_):
        return (x_ * 2 + z_ % 2, (y_ * 4 + z_ // 2) * 2 + c_)

    def remote(src, dst, ss, rs, to):
        return pltpu.make_async_remote_copy(
            src_ref=src, dst_ref=dst, send_sem=ss, recv_sem=rs, device_id=to, device_id_type=MESH)

    sib = dev(x, y, z, 1 - c)
    xpeer = [None] + [dev((x + d) % 4, y, z, c) for d in (1, 2, 3)]
    ypeer = [None] + [dev(x, (y + d) % 4, z, c) for d in (1, 2, 3)]
    zpeer = [dev(x, y, (z + 1) % 8, c), dev(x, y, (z + 7) % 8, c)]
    partner = dev(x, y, zh * 2 + c, zl)
    crossed = zl != c
    homed = zl == zh // 2
    diag = x == y

    barrier = pltpu.get_barrier_semaphore()
    for to in [sib] + xpeer[1:] + ypeer[1:] + zpeer:
        pl.semaphore_signal(barrier, inc=1, device_id=to, device_id_type=MESH)

    @pl.when(crossed)
    def _():
        pl.semaphore_signal(barrier, inc=1, device_id=partner, device_id_type=MESH)

    for b in range(4):
        @pl.when(zl * 4 + b != z)
        def _():
            pl.semaphore_signal(barrier, inc=1, device_id=dev(x, y, zl * 4 + b, c), device_id_type=MESH)

    for q in range(4):
        for p in range(2):
            @pl.when(jnp.logical_not(jnp.logical_and(diag, jnp.logical_and(y == q, c == p))))
            def _():
                pl.semaphore_signal(barrier, inc=1, device_id=dev(y, q, z, p), device_id_type=MESH)

    for cp in loads:
        cp.wait()
    ri = lax.broadcasted_iota(jnp.int32, (B, B), 0)
    ci = lax.broadcasted_iota(jnp.int32, (B, B), 1)
    colok = ci < size_ref[col]
    for s, b in enumerate(ORDER):
        rb = row * 4 + b
        ok = jnp.logical_and(colok, ri < size_ref[rb]).astype(F32)
        up = (ri + rb * B <= ci + col * B).astype(F32)
        zg[z, s * B:(s + 1) * B, :] = z_ref[b * B:(b + 1) * B, :] * (ok * up * zm_ref[0, b].astype(F32))
        hg[z, s * B:(s + 1) * B, :] = h_ref[b * B:(b + 1) * B, :] * (ok * hm_ref[0, b].astype(F32))

    pl.semaphore_wait(barrier, 21 + crossed.astype(jnp.int32) - homed.astype(jnp.int32) - diag.astype(jnp.int32))

    swap = remote(zg.at[z], sw, sw_s.at[0], sw_s.at[1], partner)

    @pl.when(crossed)
    def _():
        swap.start()

    @pl.when(jnp.logical_not(crossed))
    def _():
        sw[...] = zg[z]

    def ring(buf, ss, rs):
        made = {}

        def step(st, s):
            for d in range(2):
                if st > 0:
                    made[st - 1, s, d].wait_recv()
                if st == 3 and s % 2 != d:
                    continue
                slot = (z + 8 - st) % 8 if d == 0 else (z + st) % 8
                part = buf.at[slot, pl.ds(s * B, B)]
                cp = remote(part, part, ss.at[d, st, s], rs.at[d, st, s], zpeer[d])
                cp.start()
                made[st, s, d] = cp

        def last():
            for s in range(4):
                made[3, s, s % 2].wait_recv()

        def sent():
            for cp in made.values():
                cp.wait_send()

        return step, last, sent

    hstep, hlast, hsent = ring(hg, h_ss, h_rs)
    zstep, zlast, zsent = ring(zg, z_ss, z_rs)

    def parts(buf, hi_ref, lo_ref, dist):
        for slot in {0: [z], 4: [(z + 4) % 8]}.get(dist, [(z + dist) % 8, (z + 8 - dist) % 8]):
            hi, lo = split(buf[slot])
            hi_ref[slot] = hi
            lo_ref[slot] = lo

    for s in range(4):
        hstep(0, s)
    parts(hg, ah, al, 0)

    @pl.when(crossed)
    def _():
        swap.wait_recv()

    zrow = pl.ds(pl.multiple_of(c * 256, 256), 256)
    sends = []
    for d in (2, 1, 3, 0):
        for p in range(2):
            cp = remote(sw.at[pl.ds(p * 256, 256)], z1.at[y, zrow], z1_ss.at[d, p], z1_rs.at[y, c],
                        dev((x + d) % 4, x, z, p))
            own = jnp.logical_and(diag, c == p) if d == 0 else None
            sends.append((own, cp))
            if own is None:
                cp.start()
            else:
                pl.when(jnp.logical_not(own))(cp.start)

                @pl.when(own)
                def _():
                    z1[y, zrow, :] = sw[p * 256:(p + 1) * 256, :]

    for st in (1, 2, 3):
        for s in range(4):
            hstep(st, s)
        parts(hg, ah, al, st)
    for s in range(4):
        zstep(0, s)
    parts(zg, bh, bl, 0)
    for q in range(4):
        for p in range(2):
            @pl.when(jnp.logical_not(jnp.logical_and(diag, jnp.logical_and(y == q, c == p))))
            def _():
                remote(sw.at[pl.ds(0, 256)], z1.at[q, pl.ds(p * 256, 256)], z1_ss.at[0, 0], z1_rs.at[q, p], sib).wait_recv()

        hi, lo = split(z1[q].T)
        for m in range(CHUNKS):
            z1h[m, q * HALF:(q + 1) * HALF, :] = hi[m * HALF:(m + 1) * HALF, :]
            z1l[m, q * HALF:(q + 1) * HALF, :] = lo[m * HALF:(m + 1) * HALF, :]

    def whole(ref):
        return jnp.concatenate(
            [jnp.concatenate([ref[2 * q + half] for q in range(4)], axis=1) for half in range(2)], axis=0)

    kz = [1 - zl, zl]
    myrow = pl.ds(pl.multiple_of(y * HALF, HALF), HALF)

    def first(k, m):
        rh, rl = [jnp.concatenate([ref[2 * q + kz[k]] for q in range(4)], axis=1) for ref in (ah, al)]
        t = dot3(z1h[m], z1l[m], rh, rl, 1)
        wp[k, m, 0] = t[:, :256]
        wp[k, m, 1] = t[:, 256:]
        cp = remote(wp.at[k, m, 1 - c], cr.at[k, m], wc_ss.at[k, m], wc_rs.at[k, m], sib)
        cp.start()
        return cp

    def scatter(k, m, cp):
        cp.wait_recv()
        wc[k, m] = wp[k, m, c] + cr[k, m]
        cps = {}
        for d in (2, 1, 3):
            piece = pl.ds(pl.multiple_of(((y + d) % 4) * HALF, HALF), HALF)
            cps[d] = remote(wc.at[k, m, piece], yr.at[k, m, d - 1], wy_ss.at[k, m, d], wy_rs.at[k, m, d], ypeer[d])
            cps[d].start()
        return cps

    def spread(k, m, cps):
        for d in (1, 3, 2):
            cps[d].wait_recv()
        wt[m, kz[k], c, myrow, :] = (wc[k, m, myrow, :] + yr[k, m, 0]) + (yr[k, m, 1] + yr[k, m, 2])
        own = wt.at[m, kz[k], c, myrow]
        out = {}
        for d in (2, 1, 3):
            out[d] = remote(own, own, wa_ss.at[k, m, d], wa_rs.at[k, m, d], ypeer[d])
            out[d].start()
        out[0] = remote(own, own, wf_ss.at[k, m, 0], wf_rs.at[k, m, 0], sib)
        out[0].start()
        return out

    def forward(k, m, out):
        for d in (1, 3, 2):
            out[d].wait_recv()
            part = wt.at[m, kz[k], c, pl.ds(pl.multiple_of(((y + 4 - d) % 4) * HALF, HALF), HALF)]
            out[d + 3] = remote(part, part, wf_ss.at[k, m, d], wf_rs.at[k, m, d], sib)
            out[d + 3].start()

    c00 = first(0, 0)
    c01 = first(0, 1)
    hlast()
    parts(hg, ah, al, 4)
    s00 = scatter(0, 0, c00)
    c10 = first(1, 0)
    s01 = scatter(0, 1, c01)
    c11 = first(1, 1)
    s10 = scatter(1, 0, c10)
    o00 = spread(0, 0, s00)
    s11 = scatter(1, 1, c11)
    zstep(1, 0)
    zstep(1, 1)
    o01 = spread(0, 1, s01)
    zstep(1, 2)
    zstep(1, 3)
    parts(zg, bh, bl, 1)
    forward(0, 0, o00)
    o10 = spread(1, 0, s10)
    zstep(2, 0)
    zstep(2, 1)
    o11 = spread(1, 1, s11)
    forward(0, 1, o01)
    zstep(2, 2)
    zstep(2, 3)
    parts(zg, bh, bl, 2)
    zstep(3, 0)
    zstep(3, 1)
    forward(1, 0, o10)
    zstep(3, 2)
    zstep(3, 3)
    parts(zg, bh, bl, 3)
    zlast()
    parts(zg, bh, bl, 4)

    def second(m, outs):
        for out in outs:
            for d in (0, 4, 5, 6):
                out[d].wait_recv()
        hi, lo = split(jnp.concatenate([wt[m, half, p] for half in range(2) for p in range(2)], axis=1))
        t = dot3(hi, lo, whole(bh), whole(bl), 0)
        for q in range(4):
            u[m, q] = t[q * HALF:(q + 1) * HALF, :]
        cps = {}
        for d in (1, 3, 2):
            cps[d] = remote(u.at[m, (x + d) % 4], xr.at[m, d - 1], ux_ss.at[m, d], ux_rs.at[m, d], xpeer[d])
            cps[d].start()
        return cps

    place = (zh % 2) * 2 + zl
    away = {}

    def deliver(m, cps):
        for d in (1, 3, 2):
            cps[d].wait_recv()
        v = (u[m, x] + xr[m, 0]) + (xr[m, 1] + xr[m, 2])
        for q in range(4):
            fin[m, q] = v[:, q * B:(q + 1) * B]
            to = 2 * q + zh // 2
            cp = remote(fin.at[m, q], tr.at[place, m], fd_ss.at[m, q], fd_rs.at[m, place], dev(x, y, to, c))
            away[m, q] = to, cp

            @pl.when(to == z)
            def _():
                tr[place, m] = fin[m, q]

            @pl.when(to != z)
            def _():
                cp.start()

    u0 = second(0, (o00, o10))
    forward(1, 1, o11)
    u1 = second(1, (o01, o11))
    deliver(0, u0)
    deliver(1, u1)
    for m in range(CHUNKS):
        for b in range(4):
            @pl.when(zl * 4 + b != z)
            def _():
                remote(fin.at[0, 0], tr.at[b, m], fd_ss.at[0, 0], fd_rs.at[m, b], sib).wait_recv()

            out_ref[b * B + m * HALF:b * B + (m + 1) * HALF, :] = tr[b, m] * km_ref[0, b].astype(F32)

    hsent()
    zsent()

    @pl.when(crossed)
    def _():
        swap.wait_send()

    for own, cp in sends:
        if own is None:
            cp.wait_send()
        else:
            pl.when(jnp.logical_not(own))(cp.wait_send)
    for group in (s00, s01, s10, s11, o00, o01, o10, o11, u0, u1):
        for cp in group.values():
            cp.wait_send()
    for cp in (c00, c01, c10, c11):
        cp.wait_send()
    for to, cp in away.values():
        @pl.when(to != z)
        def _():
            cp.wait_send()


def local(hamiltonian, h_mask, factor, z_mask, k_mask, block_sizes):
    dma = pltpu.SemaphoreType.DMA
    bf = jnp.bfloat16
    flags = pltpu.SMEM((1, 4), jnp.int32)
    scratch = [
        pltpu.VMEM((512, B), F32), pltpu.VMEM((512, B), F32), flags, flags, flags,
        pltpu.SMEM((32,), jnp.int32), dma((6,)),
        pltpu.VMEM((8, 512, B), F32),
        pltpu.VMEM((8, 512, B), F32),
        pltpu.VMEM((8, 512, B), bf), pltpu.VMEM((8, 512, B), bf),
        pltpu.VMEM((8, 512, B), bf), pltpu.VMEM((8, 512, B), bf),
        pltpu.VMEM((512, B), F32),
        pltpu.VMEM((4, 512, B), F32),
        pltpu.VMEM((CHUNKS, 256, 512), bf), pltpu.VMEM((CHUNKS, 256, 512), bf),
        pltpu.VMEM((2, CHUNKS, 2, 256, 256), F32),
        pltpu.VMEM((2, CHUNKS, 256, 256), F32),
        pltpu.VMEM((2, CHUNKS, 256, 256), F32),
        pltpu.VMEM((2, CHUNKS, 3, HALF, 256), F32),
        pltpu.VMEM((CHUNKS, 2, 2, 256, 256), F32),
        pltpu.VMEM((CHUNKS, 4, HALF, 512), F32),
        pltpu.VMEM((CHUNKS, 3, HALF, 512), F32),
        pltpu.VMEM((CHUNKS, 4, HALF, B), F32),
        pltpu.VMEM((4, CHUNKS, HALF, B), F32),
        dma((2, 4, 4)), dma((2, 4, 4)), dma((2, 4, 4)), dma((2, 4, 4)),
        dma((2,)), dma((4, 2)), dma((4, 2)),
        dma((2, 2)), dma((2, 2)), dma((2, 2, 4)), dma((2, 2, 4)), dma((2, 2, 4)), dma((2, 2, 4)),
        dma((2, 2, 4)), dma((2, 2, 4)), dma((2, 4)), dma((2, 4)), dma((2, 4)), dma((2, 4)),
    ]
    hbm = pl.BlockSpec(memory_space=pltpu.HBM)
    return pl.pallas_call(
        kernel,
        out_shape=jax.ShapeDtypeStruct((512, B), F32),
        in_specs=[hbm] * 6,
        out_specs=pl.BlockSpec(memory_space=pltpu.VMEM),
        scratch_shapes=scratch,
        compiler_params=pltpu.CompilerParams(
            collective_id=0, has_side_effects=True, vmem_limit_bytes=48 << 20),
        name="congruence",
    )(*[pltpu.with_memory_space_constraint(v, pltpu.HBM) for v in (
        hamiltonian, h_mask.reshape(1, 4), factor, z_mask.reshape(1, 4), k_mask.reshape(1, 4), block_sizes)])


def solution(mesh):
    placed = (
        P("row", "col"),
        P("row", "col"),
        P("row", "col"),
        P("row", "col"),
        P("row", "col"),
        P(),
    )
    return jax.shard_map(
        local, mesh=mesh, in_specs=placed, out_specs=P("row", "col"), check_vma=False
    )
```

```python
import jax
import jax.numpy as jnp
from jax import lax
from jax.experimental import pallas as pl
from jax.experimental.pallas import tpu as pltpu
from jax.sharding import PartitionSpec as P

B = 128
MESH = pl.DeviceIdType.MESH
ORDER = (0, 2, 1, 3)
F32 = jnp.float32
CHUNKS = 2
HALF = B // CHUNKS


def split(v):
    hi = v.astype(jnp.bfloat16)
    return hi, (v - hi.astype(F32)).astype(jnp.bfloat16)


def when(cond, act):
    if cond is None:
        act()
    else:
        pl.when(cond)(act)


def dot3(ah, al, bh, bl, axis):
    return lax.dot_general(
        jnp.concatenate([ah, ah, al], axis=1), jnp.concatenate([bh, bl, bh], axis=axis),
        (((1,), (axis,)), ((), ())), preferred_element_type=F32)


def kernel(h_hbm, hm_hbm, z_hbm, zm_hbm, km_hbm, size_hbm, out_ref,
           h_ref, z_ref, hm_ref, zm_ref, km_ref, size_ref, in_s,
           hg, zg, ah, al, bh, bl, sw, z1, z1h, z1l, wp, cr, wc, yr, wt, wh, wl, u, xr, fin, fint, tr,
           h_ss, h_rs, z_ss, z_rs, sw_s, z1_ss, z1_rs,
           wc_ss, wc_rs, wy_ss, wy_rs, wa_ss, wa_rs, wf_ss, wf_rs, ux_ss, ux_rs, fd_ss, fm_ss, fd_rs):
    row = lax.axis_index("row")
    col = lax.axis_index("col")
    x, zl = row // 2, row % 2
    y, zh, c = col // 8, (col // 2) % 4, col % 2
    z = zh * 2 + zl

    loads = [
        pltpu.make_async_copy(src, dst, in_s.at[i])
        for i, (src, dst) in enumerate([
            (size_hbm, size_ref), (zm_hbm, zm_ref), (z_hbm, z_ref), (hm_hbm, hm_ref), (h_hbm, h_ref), (km_hbm, km_ref)])
    ]
    for cp in loads:
        cp.start()

    def dev(x_, y_, z_, c_):
        return (x_ * 2 + z_ % 2, (y_ * 4 + z_ // 2) * 2 + c_)

    def remote(src, dst, ss, rs, to):
        return pltpu.make_async_remote_copy(
            src_ref=src, dst_ref=dst, send_sem=ss, recv_sem=rs, device_id=to, device_id_type=MESH)

    sib = dev(x, y, z, 1 - c)
    xpeer = [None] + [dev((x + d) % 4, y, z, c) for d in (1, 2, 3)]
    ypeer = [None] + [dev(x, (y + d) % 4, z, c) for d in (1, 2, 3)]
    zpeer = [dev(x, y, (z + 1) % 8, c), dev(x, y, (z + 7) % 8, c)]
    partner = dev(x, y, zh * 2 + c, zl)
    crossed = zl != c
    homed = zl == zh // 2
    diag = x == y

    barrier = pltpu.get_barrier_semaphore()
    for to in [sib] + xpeer[1:] + ypeer[1:] + zpeer:
        pl.semaphore_signal(barrier, inc=1, device_id=to, device_id_type=MESH)

    @pl.when(crossed)
    def _():
        pl.semaphore_signal(barrier, inc=1, device_id=partner, device_id_type=MESH)

    lower = x >= y
    for p in range(2):
        @pl.when(x < y)
        def _():
            pl.semaphore_signal(barrier, inc=1, device_id=dev(y, x, 2 * zh + c, p), device_id_type=MESH)

    for b in range(4):
        @pl.when(jnp.logical_and(lower, zl * 4 + b != z))
        def _():
            pl.semaphore_signal(barrier, inc=1, device_id=dev(x, y, zl * 4 + b, c), device_id_type=MESH)

    for q in range(4):
        for p in range(2):
            @pl.when(jnp.logical_not(jnp.logical_and(diag, jnp.logical_and(y == q, c == p))))
            def _():
                pl.semaphore_signal(barrier, inc=1, device_id=dev(y, q, z, p), device_id_type=MESH)

    for cp in loads:
        cp.wait()
    ri = lax.broadcasted_iota(jnp.int32, (B, B), 0)
    ci = lax.broadcasted_iota(jnp.int32, (B, B), 1)
    colok = ci < size_ref[col]
    for s, b in enumerate(ORDER):
        rb = row * 4 + b
        ok = jnp.logical_and(colok, ri < size_ref[rb]).astype(F32)
        up = (ri + rb * B <= ci + col * B).astype(F32)
        zg[z, s * B:(s + 1) * B, :] = z_ref[b * B:(b + 1) * B, :] * (ok * up * zm_ref[0, b].astype(F32))
        hg[z, s * B:(s + 1) * B, :] = h_ref[b * B:(b + 1) * B, :] * (ok * hm_ref[0, b].astype(F32))

    greets = jnp.where(lower, 4 - homed.astype(jnp.int32), 0) + jnp.where(x > y, 2, 0)
    pl.semaphore_wait(barrier, 17 + crossed.astype(jnp.int32) - diag.astype(jnp.int32) + greets)

    swap = remote(zg.at[z], sw, sw_s.at[0], sw_s.at[1], partner)

    @pl.when(crossed)
    def _():
        swap.start()

    @pl.when(jnp.logical_not(crossed))
    def _():
        sw[...] = zg[z]

    def ring(buf, ss, rs):
        made = {}

        def step(st, s):
            for d in range(2):
                if st > 0:
                    made[st - 1, s, d].wait_recv()
                if st == 3 and s % 2 != d:
                    continue
                slot = (z + 8 - st) % 8 if d == 0 else (z + st) % 8
                part = buf.at[slot, pl.ds(s * B, B)]
                cp = remote(part, part, ss.at[d, st, s], rs.at[d, st, s], zpeer[d])
                cp.start()
                made[st, s, d] = cp

        def last(subs):
            for s in subs:
                made[3, s, s % 2].wait_recv()

        def sent():
            for cp in made.values():
                cp.wait_send()

        return step, last, sent

    hstep, hlast, hsent = ring(hg, h_ss, h_rs)
    zstep, zlast, zsent = ring(zg, z_ss, z_rs)

    def parts(buf, hi_ref, lo_ref, dist, rows=slice(0, 512)):
        for slot in {0: [z], 4: [(z + 4) % 8]}.get(dist, [(z + dist) % 8, (z + 8 - dist) % 8]):
            hi, lo = split(buf[slot, rows, :])
            hi_ref[slot, rows, :] = hi
            lo_ref[slot, rows, :] = lo

    pair = (slice(0, 256), slice(256, 512))
    for s in (0, 1, 2):
        hstep(0, s)
    parts(hg, ah, al, 0)

    @pl.when(crossed)
    def _():
        swap.wait_recv()

    zrow = pl.ds(pl.multiple_of(c * 256, 256), 256)
    sends = []
    for d in (2, 1, 3, 0):
        for p in range(2):
            cp = remote(sw.at[pl.ds(p * 256, 256)], z1.at[y, zrow], z1_ss.at[d, p], z1_rs.at[y, c],
                        dev((x + d) % 4, x, z, p))
            own = jnp.logical_and(diag, c == p) if d == 0 else None
            sends.append((own, cp))
            if own is None:
                cp.start()
            else:
                pl.when(jnp.logical_not(own))(cp.start)

                @pl.when(own)
                def _():
                    z1[y, zrow, :] = sw[p * 256:(p + 1) * 256, :]

    hstep(1, 0)
    hstep(1, 1)
    parts(hg, ah, al, 1, pair[0])
    hstep(0, 3)
    hstep(2, 0)
    hstep(2, 1)
    parts(hg, ah, al, 2, pair[0])
    hstep(1, 2)
    hstep(3, 0)
    hstep(3, 1)
    parts(hg, ah, al, 3, pair[0])
    hstep(1, 3)
    parts(hg, ah, al, 1, pair[1])
    hstep(2, 2)
    for q in range(4):
        for p in range(2):
            @pl.when(jnp.logical_not(jnp.logical_and(diag, jnp.logical_and(y == q, c == p))))
            def _():
                remote(sw.at[pl.ds(0, 256)], z1.at[q, pl.ds(p * 256, 256)], z1_ss.at[0, 0], z1_rs.at[q, p], sib).wait_recv()

        hi, lo = split(z1[q].T)
        for m in range(CHUNKS):
            z1h[m, q * HALF:(q + 1) * HALF, :] = hi[m * HALF:(m + 1) * HALF, :]
            z1l[m, q * HALF:(q + 1) * HALF, :] = lo[m * HALF:(m + 1) * HALF, :]

    hlast((0, 1))
    parts(hg, ah, al, 4, pair[0])
    myrow = pl.ds(pl.multiple_of(y * HALF, HALF), HALF)

    def first(k, m):
        rh, rl = [
            jnp.concatenate(
                [jnp.concatenate([ref[2 * q + half, pair[k], :] for q in range(4)], axis=1) for half in range(2)], axis=0)
            for ref in (ah, al)]
        t = dot3(z1h[m], z1l[m], rh, rl, 1)
        wp[k, m, 0] = t[:, :256]
        wp[k, m, 1] = t[:, 256:]
        cp = remote(wp.at[k, m, 1 - c], cr.at[k, m], wc_ss.at[k, m], wc_rs.at[k, m], sib)
        cp.start()
        return cp

    def scatter(k, m, cp):
        cp.wait_recv()
        wc[k, m] = wp[k, m, c] + cr[k, m]
        cps = {}
        for d in (2, 1, 3):
            piece = pl.ds(pl.multiple_of(((y + d) % 4) * HALF, HALF), HALF)
            cond = jnp.logical_and(y + d < 4, y + d >= x)
            cps[d] = cond, remote(
                wc.at[k, m, piece], yr.at[k, m, d - 1], wy_ss.at[k, m, d], wy_rs.at[k, m, d], ypeer[d])
            when(cond, cps[d][1].start)
        return cps

    def spread(k, m, cps):
        wt[m, k, c, myrow, :] = wc[k, m, myrow, :]
        for d in (1, 3, 2):
            @pl.when(jnp.logical_and(d <= y, x <= y))
            def _():
                cps[d][1].wait_recv()
                wt[m, k, c, myrow, :] += yr[k, m, d - 1]

        own = wt.at[m, k, c, myrow]
        out = {}
        for d in (2, 1, 3):
            cond = jnp.logical_and(y + d >= 4, y + d - 4 >= x)
            out[d] = cond, remote(own, own, wa_ss.at[k, m, d], wa_rs.at[k, m, d], ypeer[d])
            when(cond, out[d][1].start)
        out[0] = None, remote(own, own, wf_ss.at[k, m, 0], wf_rs.at[k, m, 0], sib)
        out[0][1].start()
        return out

    def forward(k, m, out):
        for d in (1, 3, 2):
            part = wt.at[m, k, c, pl.ds(pl.multiple_of(((y + 4 - d) % 4) * HALF, HALF), HALF)]
            cond = jnp.logical_and(d > y, x <= y)
            out[d + 3] = cond, remote(part, part, wf_ss.at[k, m, d], wf_rs.at[k, m, d], sib)

            @pl.when(cond)
            def _():
                out[d][1].wait_recv()
                out[d + 3][1].start()

    def gathered(k, m, out):
        for d in (0, 4, 5, 6):
            when(out[d][0], out[d][1].wait_recv)
        for half in range(2):
            hi, lo = split(wt[m, k, half])
            at = (k * 2 + half) * 256
            for q in range(4):
                wh[q * B + m * HALF:q * B + (m + 1) * HALF, at:at + 256] = hi[q * HALF:(q + 1) * HALF, :]
                wl[q * B + m * HALF:q * B + (m + 1) * HALF, at:at + 256] = lo[q * HALF:(q + 1) * HALF, :]

    c00 = first(0, 0)
    hstep(2, 3)
    c01 = first(0, 1)
    zstep(0, 0)
    hstep(3, 2)
    s00 = scatter(0, 0, c00)
    zstep(0, 1)
    parts(hg, ah, al, 2, pair[1])
    s01 = scatter(0, 1, c01)
    hstep(3, 3)
    zstep(0, 2)
    zstep(0, 3)
    parts(hg, ah, al, 3, pair[1])
    parts(zg, bh, bl, 0)
    hlast((2, 3))
    parts(hg, ah, al, 4, pair[1])
    c10 = first(1, 0)
    o00 = spread(0, 0, s00)
    zstep(1, 0)
    c11 = first(1, 1)
    zstep(1, 1)
    s10 = scatter(1, 0, c10)
    o01 = spread(0, 1, s01)
    zstep(1, 2)
    s11 = scatter(1, 1, c11)
    zstep(1, 3)
    parts(zg, bh, bl, 1)
    forward(0, 0, o00)
    zstep(2, 0)
    zstep(2, 1)
    o10 = spread(1, 0, s10)
    gathered(0, 0, o00)
    zstep(2, 2)
    zstep(2, 3)
    parts(zg, bh, bl, 2)
    forward(0, 1, o01)
    zstep(3, 0)
    gathered(0, 1, o01)
    zstep(3, 1)
    o11 = spread(1, 1, s11)
    zstep(3, 2)
    zstep(3, 3)
    parts(zg, bh, bl, 3)
    forward(1, 0, o10)
    gathered(1, 0, o10)
    forward(1, 1, o11)
    gathered(1, 1, o11)

    shift = zl * 2 + 3
    near = [zh, (zh + shift) % 4, (zh + 4 - shift % 4) % 4, (zh + 2) % 4]

    def second(js):
        rh, rl = [
            jnp.concatenate(
                [jnp.concatenate([ref[2 * near[j] + half, pair[k], :] for k in range(2) for half in range(2)], axis=0)
                 for j in js], axis=1)
            for ref in (bh, bl)]
        t = dot3(wh[...], wl[...], rh, rl, 0)
        outs = []
        for i, j in enumerate(js):
            for q in range(4):
                u[j, q] = t[q * B:(q + 1) * B, i * B:(i + 1) * B]
            cps = {}
            for d in (2, 1, 3):
                q = (x + d) % 4
                cond = jnp.logical_and(x <= y, q >= y)
                cps[d] = cond, remote(u.at[j, q], xr.at[j, d - 1], ux_ss.at[j, d], ux_rs.at[j, d], xpeer[d])
                when(cond, cps[d][1].start)
            outs.append(cps)
        return outs

    place = (zh % 2) * 2 + zl
    away = {}

    def deliver(j, cps):
        fin[j] = jnp.where(diag, u[j, x], 0.0)
        for d in (1, 3, 2):
            @pl.when(jnp.logical_and(lower, (x + 4 - d) % 4 <= y))
            def _():
                cps[d][1].wait_recv()
                fin[j] += xr[j, d - 1]

        to = 2 * near[j] + zh // 2
        slot = (near[j] % 2) * 2 + c
        away[j] = [
            (jnp.logical_and(lower, to != z),
             remote(fin.at[j], tr.at[place], fd_ss.at[j], fd_rs.at[place], dev(x, y, to, c))),
            (x > y,
             remote(fint.at[j], tr.at[slot], fm_ss.at[j], fd_rs.at[slot], dev(y, x, 2 * zh + near[j] // 2, zl))),
        ]
        when(away[j][0][0], away[j][0][1].start)

        @pl.when(x > y)
        def _():
            fint[j] = fin[j].T
            away[j][1][1].start()

        @pl.when(jnp.logical_and(lower, to == z))
        def _():
            tr[place] = fin[j]

    u0, u1 = second((0, 1))
    (u2,) = second((2,))
    deliver(0, u0)
    deliver(1, u1)
    zlast(range(4))
    parts(zg, bh, bl, 4)
    (u3,) = second((3,))
    deliver(2, u2)
    deliver(3, u3)
    for b in range(4):
        @pl.when(jnp.logical_not(jnp.logical_and(lower, zl * 4 + b == z)))
        def _():
            remote(fin.at[0], tr.at[b], fd_ss.at[0], fd_rs.at[b], sib).wait_recv()

        out_ref[b * B:(b + 1) * B, :] = tr[b] * km_ref[0, b].astype(F32)

    hsent()
    zsent()

    @pl.when(crossed)
    def _():
        swap.wait_send()

    for own, cp in sends:
        if own is None:
            cp.wait_send()
        else:
            pl.when(jnp.logical_not(own))(cp.wait_send)
    for group in (s00, s01, s10, s11, o00, o01, o10, o11, u0, u1, u2, u3):
        for cond, cp in group.values():
            when(cond, cp.wait_send)
    for cp in (c00, c01, c10, c11):
        cp.wait_send()
    for group in away.values():
        for cond, cp in group:
            when(cond, cp.wait_send)


def local(hamiltonian, h_mask, factor, z_mask, k_mask, block_sizes):
    dma = pltpu.SemaphoreType.DMA
    bf = jnp.bfloat16
    flags = pltpu.SMEM((1, 4), jnp.int32)
    scratch = [
        pltpu.VMEM((512, B), F32), pltpu.VMEM((512, B), F32), flags, flags, flags,
        pltpu.SMEM((32,), jnp.int32), dma((6,)),
        pltpu.VMEM((8, 512, B), F32),
        pltpu.VMEM((8, 512, B), F32),
        pltpu.VMEM((8, 512, B), bf), pltpu.VMEM((8, 512, B), bf),
        pltpu.VMEM((8, 512, B), bf), pltpu.VMEM((8, 512, B), bf),
        pltpu.VMEM((512, B), F32),
        pltpu.VMEM((4, 512, B), F32),
        pltpu.VMEM((CHUNKS, 256, 512), bf), pltpu.VMEM((CHUNKS, 256, 512), bf),
        pltpu.VMEM((2, CHUNKS, 2, 256, 256), F32),
        pltpu.VMEM((2, CHUNKS, 256, 256), F32),
        pltpu.VMEM((2, CHUNKS, 256, 256), F32),
        pltpu.VMEM((2, CHUNKS, 3, HALF, 256), F32),
        pltpu.VMEM((CHUNKS, 2, 2, 256, 256), F32),
        pltpu.VMEM((512, 1024), bf), pltpu.VMEM((512, 1024), bf),
        pltpu.VMEM((4, 4, B, B), F32),
        pltpu.VMEM((4, 3, B, B), F32),
        pltpu.VMEM((4, B, B), F32), pltpu.VMEM((4, B, B), F32),
        pltpu.VMEM((4, B, B), F32),
        dma((2, 4, 4)), dma((2, 4, 4)), dma((2, 4, 4)), dma((2, 4, 4)),
        dma((2,)), dma((4, 2)), dma((4, 2)),
        dma((2, 2)), dma((2, 2)), dma((2, 2, 4)), dma((2, 2, 4)), dma((2, 2, 4)), dma((2, 2, 4)),
        dma((2, 2, 4)), dma((2, 2, 4)), dma((4, 4)), dma((4, 4)), dma((4,)), dma((4,)), dma((4,)),
    ]
    hbm = pl.BlockSpec(memory_space=pltpu.HBM)
    return pl.pallas_call(
        kernel,
        out_shape=jax.ShapeDtypeStruct((512, B), F32),
        in_specs=[hbm] * 6,
        out_specs=pl.BlockSpec(memory_space=pltpu.VMEM),
        scratch_shapes=scratch,
        compiler_params=pltpu.CompilerParams(
            collective_id=0, has_side_effects=True, vmem_limit_bytes=48 << 20),
        name="congruence",
    )(*[pltpu.with_memory_space_constraint(v, pltpu.HBM) for v in (
        hamiltonian, h_mask.reshape(1, 4), factor, z_mask.reshape(1, 4), k_mask.reshape(1, 4), block_sizes)])


def solution(mesh):
    placed = (
        P("row", "col"),
        P("row", "col"),
        P("row", "col"),
        P("row", "col"),
        P("row", "col"),
        P(),
    )
    return jax.shard_map(
        local, mesh=mesh, in_specs=placed, out_specs=P("row", "col"), check_vma=False
    )
```

```python
import jax
import jax.numpy as jnp
from jax import lax
from jax.experimental import pallas as pl
from jax.experimental.pallas import tpu as pltpu
from jax.sharding import PartitionSpec as P

B = 128
MESH = pl.DeviceIdType.MESH
ORDER = (0, 2, 1, 3)
F32 = jnp.float32
CHUNKS = 2
HALF = B // CHUNKS
OWNER = ((0, 0, 1, 2), (0, 0, 1, 3))


def split(v):
    hi = v.astype(jnp.bfloat16)
    return hi, (v - hi.astype(F32)).astype(jnp.bfloat16)


def when(cond, act):
    if cond is None:
        act()
    else:
        pl.when(cond)(act)


def dot3(ah, al, bh, bl, axis):
    return lax.dot_general(
        jnp.concatenate([ah, ah, al], axis=1), jnp.concatenate([bh, bl, bh], axis=axis),
        (((1,), (axis,)), ((), ())), preferred_element_type=F32)


def kernel(h_hbm, hm_hbm, z_hbm, zm_hbm, km_hbm, size_hbm, out_ref,
           h_ref, z_ref, hm_ref, zm_ref, km_ref, size_ref, in_s,
           hg, zg, ah, al, bh, bl, sw, z1, z1h, z1l, wp, cr, wc, yr, wt, wh, wl, u, xr, fin, fint, tr,
           h_ss, h_rs, z_ss, z_rs, sw_s, z1_ss, z1_rs,
           wc_ss, wc_rs, wy_ss, wy_rs, wa_ss, wa_rs, wf_ss, wf_rs, ux_ss, ux_rs, fd_ss, fm_ss, fd_rs):
    row = lax.axis_index("row")
    col = lax.axis_index("col")
    x, zl = row // 2, row % 2
    y, zh, c = col // 8, (col // 2) % 4, col % 2
    z = zh * 2 + zl

    loads = [
        pltpu.make_async_copy(src, dst, in_s.at[i])
        for i, (src, dst) in enumerate([
            (size_hbm, size_ref), (zm_hbm, zm_ref), (z_hbm, z_ref), (hm_hbm, hm_ref), (h_hbm, h_ref), (km_hbm, km_ref)])
    ]
    for cp in loads:
        cp.start()

    def dev(x_, y_, z_, c_):
        return (x_ * 2 + z_ % 2, (y_ * 4 + z_ // 2) * 2 + c_)

    def remote(src, dst, ss, rs, to):
        return pltpu.make_async_remote_copy(
            src_ref=src, dst_ref=dst, send_sem=ss, recv_sem=rs, device_id=to, device_id_type=MESH)

    sib = dev(x, y, z, 1 - c)
    xpeer = [None] + [dev((x + d) % 4, y, z, c) for d in (1, 2, 3)]
    ypeer = [dev(x, (y + d) % 4, z, c) for d in (1, 2, 3)]
    zpeer = [dev(x, y, (z + 1) % 8, c), dev(x, y, (z + 7) % 8, c)]
    partner = dev(x, y, zh * 2 + c, zl)
    crossed = zl != c
    homed = zl == zh // 2
    diag = x == y

    barrier = pltpu.get_barrier_semaphore()
    for to in [sib] + xpeer[1:] + ypeer + zpeer:
        pl.semaphore_signal(barrier, inc=1, device_id=to, device_id_type=MESH)

    @pl.when(crossed)
    def _():
        pl.semaphore_signal(barrier, inc=1, device_id=partner, device_id_type=MESH)

    lower = x >= y
    for p in range(2):
        @pl.when(x < y)
        def _():
            pl.semaphore_signal(barrier, inc=1, device_id=dev(y, x, 2 * zh + c, p), device_id_type=MESH)

    for b in range(4):
        @pl.when(jnp.logical_and(lower, zl * 4 + b != z))
        def _():
            pl.semaphore_signal(barrier, inc=1, device_id=dev(x, y, zl * 4 + b, c), device_id_type=MESH)

    for q in range(4):
        for p in range(2):
            @pl.when(jnp.logical_not(jnp.logical_and(diag, jnp.logical_and(y == q, c == p))))
            def _():
                pl.semaphore_signal(barrier, inc=1, device_id=dev(y, q, z, p), device_id_type=MESH)

    for cp in loads:
        cp.wait()
    ri = lax.broadcasted_iota(jnp.int32, (B, B), 0)
    ci = lax.broadcasted_iota(jnp.int32, (B, B), 1)
    colok = ci < size_ref[col]
    for s, b in enumerate(ORDER):
        rb = row * 4 + b
        ok = jnp.logical_and(colok, ri < size_ref[rb]).astype(F32)
        up = (ri + rb * B <= ci + col * B).astype(F32)
        zg[z, s * B:(s + 1) * B, :] = z_ref[b * B:(b + 1) * B, :] * (ok * up * zm_ref[0, b].astype(F32))
        hg[z, s * B:(s + 1) * B, :] = h_ref[b * B:(b + 1) * B, :] * (ok * hm_ref[0, b].astype(F32))

    greets = jnp.where(lower, 4 - homed.astype(jnp.int32), 0) + jnp.where(x > y, 2, 0)
    pl.semaphore_wait(barrier, 17 + crossed.astype(jnp.int32) - diag.astype(jnp.int32) + greets)

    swap = remote(zg.at[z], sw, sw_s.at[0], sw_s.at[1], partner)

    @pl.when(crossed)
    def _():
        swap.start()

    @pl.when(jnp.logical_not(crossed))
    def _():
        sw[...] = zg[z]

    def ring(buf, ss, rs):
        made = {}

        def step(st, s):
            for d in range(2):
                if st > 0:
                    made[st - 1, s, d].wait_recv()
                if st == 3 and s % 2 != d:
                    continue
                slot = (z + 8 - st) % 8 if d == 0 else (z + st) % 8
                part = buf.at[slot, pl.ds(s * B, B)]
                cp = remote(part, part, ss.at[d, st, s], rs.at[d, st, s], zpeer[d])
                cp.start()
                made[st, s, d] = cp

        def last(subs):
            for s in subs:
                made[3, s, s % 2].wait_recv()

        def sent():
            for cp in made.values():
                cp.wait_send()

        return step, last, sent

    hstep, hlast, hsent = ring(hg, h_ss, h_rs)
    zstep, zlast, zsent = ring(zg, z_ss, z_rs)

    def parts(buf, hi_ref, lo_ref, dist, rows=slice(0, 512)):
        for slot in {0: [z], 4: [(z + 4) % 8]}.get(dist, [(z + dist) % 8, (z + 8 - dist) % 8]):
            hi, lo = split(buf[slot, rows, :])
            hi_ref[slot, rows, :] = hi
            lo_ref[slot, rows, :] = lo

    pair = (slice(0, 256), slice(256, 512))
    for s in range(4):
        hstep(0, s)
    parts(hg, ah, al, 0)

    @pl.when(crossed)
    def _():
        swap.wait_recv()

    zrow = pl.ds(pl.multiple_of(c * 256, 256), 256)
    sends = []
    for d in (2, 1, 3, 0):
        for p in range(2):
            cp = remote(sw.at[pl.ds(p * 256, 256)], z1.at[y, zrow], z1_ss.at[d, p], z1_rs.at[y, c],
                        dev((x + d) % 4, x, z, p))
            own = jnp.logical_and(diag, c == p) if d == 0 else None
            sends.append((own, cp))
            if own is None:
                cp.start()
            else:
                pl.when(jnp.logical_not(own))(cp.start)

                @pl.when(own)
                def _():
                    z1[y, zrow, :] = sw[p * 256:(p + 1) * 256, :]

    for st in (1, 2, 3):
        for s in range(4):
            hstep(st, s)
        parts(hg, ah, al, st)
    for s in range(4):
        zstep(0, s)
    parts(zg, bh, bl, 0)
    for q in range(4):
        for p in range(2):
            @pl.when(jnp.logical_not(jnp.logical_and(diag, jnp.logical_and(y == q, c == p))))
            def _():
                remote(sw.at[pl.ds(0, 256)], z1.at[q, pl.ds(p * 256, 256)], z1_ss.at[0, 0], z1_rs.at[q, p], sib).wait_recv()

        hi, lo = split(z1[q].T)
        for m in range(CHUNKS):
            z1h[m, q * HALF:(q + 1) * HALF, :] = hi[m * HALF:(m + 1) * HALF, :]
            z1l[m, q * HALF:(q + 1) * HALF, :] = lo[m * HALF:(m + 1) * HALF, :]

    def both(*conds):
        out = conds[0]
        for cond in conds[1:]:
            out = jnp.logical_and(out, cond)
        return out

    kz = [1 - zl, zl]
    uses = [both(x <= y, y <= q) for q in range(4)]

    def first(k, m):
        rh, rl = [jnp.concatenate([ref[2 * q + kz[k]] for q in range(4)], axis=1) for ref in (ah, al)]
        t = dot3(z1h[m], z1l[m], rh, rl, 1)
        wp[k, m, 0] = t[:, :256]
        wp[k, m, 1] = t[:, 256:]
        cp = remote(wp.at[k, m, 1 - c], cr.at[k, m], wc_ss.at[k, m], wc_rs.at[k, m], sib)
        cp.start()
        return cp

    def scatter(k, m, cp):
        cp.wait_recv()
        wc[k, m] = wp[k, m, c] + cr[k, m]
        cps = {}
        for q in (3, 2, 1):
            for src in range(q + 1):
                to = OWNER[m][q]
                if src != to:
                    cond = both(y == src, x <= q)
                    cp = remote(wc.at[k, m, pl.ds(q * HALF, HALF)], yr.at[k, m, q, src],
                                wy_ss.at[k, m, q, src], wy_rs.at[k, m, q, src], dev(x, to, z, c))
                    cps[q, src] = cond, cp
                    when(cond, cp.start)
        return cps

    def spread(k, m, cps):
        out = {}
        for q in (3, 2, 1, 0):
            rows = pl.ds(q * HALF, HALF)
            mine = both(y == OWNER[m][q], x <= q)
            own = wt.at[m, k, c, rows]

            @pl.when(mine)
            def _():
                wt[m, k, c, rows, :] = wc[k, m, rows, :]
                for src in range(q + 1):
                    if src != OWNER[m][q]:
                        cps[q, src][1].wait_recv()
                        wt[m, k, c, rows, :] += yr[k, m, q, src]

            for to in range(q + 1):
                if to != OWNER[m][q]:
                    cond = both(mine, x <= to)
                    out[q, to] = cond, remote(own, own, wa_ss.at[k, m, q, to], wa_rs.at[k, m, q], dev(x, to, z, c))
                    when(cond, out[q, to][1].start)
            out[q, 4] = uses[q], remote(own, own, wf_ss.at[k, m, q], wf_rs.at[k, m, q], sib)
            when(both(mine, uses[q]), out[q, 4][1].start)
        return out

    def forward(k, m, out):
        for q in (3, 2, 1):
            @pl.when(both(uses[q], y != OWNER[m][q]))
            def _():
                out[q, q if q != OWNER[m][q] else 0][1].wait_recv()
                out[q, 4][1].start()

    def gathered(k, m, out):
        for q in range(4):
            when(uses[q], out[q, 4][1].wait_recv)
        for half in range(2):
            hi, lo = split(wt[m, k, half])
            at = (k * 2 + half) * 256
            wh[m, :, at:at + 256] = hi
            wl[m, :, at:at + 256] = lo

    shift = zl * 2 + 3
    near = [zh, (zh + shift) % 4, (zh + 4 - shift % 4) % 4, (zh + 2) % 4]

    def second(js, m):
        rh, rl = [
            jnp.concatenate(
                [jnp.concatenate([ref[2 * near[j] + kz[k], pair[half], :] for k in range(2) for half in range(2)], axis=0)
                 for j in js], axis=1)
            for ref in (bh, bl)]
        t = dot3(wh[m], wl[m], rh, rl, 0)
        for i, j in enumerate(js):
            for q in range(4):
                u[j, m, q] = t[q * HALF:(q + 1) * HALF, i * B:(i + 1) * B]
            for d in (2, 1, 3):
                q = (x + d) % 4
                cond = jnp.logical_and(x <= y, q >= y)
                cp = remote(u.at[j, m, q], xr.at[j, m, d - 1], ux_ss.at[j, m, d], ux_rs.at[j, m, d], xpeer[d])
                scattered[j, m, d] = cond, cp
                when(cond, cp.start)

    scattered = {}
    place = (zh % 2) * 2 + zl
    away = {}

    def deliver(j):
        for m in range(CHUNKS):
            rows = slice(m * HALF, (m + 1) * HALF)
            fin[j, rows, :] = jnp.where(diag, u[j, m, x], 0.0)
            for d in (1, 3, 2):
                @pl.when(jnp.logical_and(lower, (x + 4 - d) % 4 <= y))
                def _():
                    scattered[j, m, d][1].wait_recv()
                    fin[j, rows, :] += xr[j, m, d - 1]

        to = 2 * near[j] + zh // 2
        slot = (near[j] % 2) * 2 + c
        away[j] = [
            (jnp.logical_and(lower, to != z),
             remote(fin.at[j], tr.at[place], fd_ss.at[j], fd_rs.at[place], dev(x, y, to, c))),
            (x > y,
             remote(fint.at[j], tr.at[slot], fm_ss.at[j], fd_rs.at[slot], dev(y, x, 2 * zh + near[j] // 2, zl))),
        ]
        when(away[j][0][0], away[j][0][1].start)

        @pl.when(x > y)
        def _():
            fint[j] = fin[j].T
            away[j][1][1].start()

        @pl.when(jnp.logical_and(lower, to == z))
        def _():
            tr[place] = fin[j]

    c00 = first(0, 0)
    c01 = first(0, 1)
    s00 = scatter(0, 0, c00)
    s01 = scatter(0, 1, c01)
    hlast(range(4))
    parts(hg, ah, al, 4)
    c10 = first(1, 0)
    c11 = first(1, 1)
    zstep(1, 0)
    s10 = scatter(1, 0, c10)
    o00 = spread(0, 0, s00)
    s11 = scatter(1, 1, c11)
    o01 = spread(0, 1, s01)
    zstep(1, 1)
    zstep(1, 2)
    zstep(1, 3)
    parts(zg, bh, bl, 1)
    forward(0, 0, o00)
    forward(0, 1, o01)
    o10 = spread(1, 0, s10)
    zstep(2, 0)
    zstep(2, 1)
    o11 = spread(1, 1, s11)
    gathered(0, 0, o00)
    gathered(0, 1, o01)
    zstep(2, 2)
    zstep(2, 3)
    parts(zg, bh, bl, 2)
    forward(1, 0, o10)
    gathered(1, 0, o10)
    second((0, 1), 0)
    forward(1, 1, o11)
    gathered(1, 1, o11)
    second((0, 1), 1)
    zstep(3, 0)
    zstep(3, 1)
    zstep(3, 2)
    zstep(3, 3)
    parts(zg, bh, bl, 3)
    second((2,), 0)
    second((2,), 1)
    deliver(0)
    deliver(1)
    zlast(range(4))
    parts(zg, bh, bl, 4)
    second((3,), 0)
    second((3,), 1)
    deliver(2)
    deliver(3)
    for b in range(4):
        @pl.when(jnp.logical_not(jnp.logical_and(lower, zl * 4 + b == z)))
        def _():
            remote(fin.at[0], tr.at[b], fd_ss.at[0], fd_rs.at[b], sib).wait_recv()

        out_ref[b * B:(b + 1) * B, :] = tr[b] * km_ref[0, b].astype(F32)

    hsent()
    zsent()

    @pl.when(crossed)
    def _():
        swap.wait_send()

    for own, cp in sends:
        if own is None:
            cp.wait_send()
        else:
            pl.when(jnp.logical_not(own))(cp.wait_send)
    for group in (s00, s01, s10, s11, o00, o01, o10, o11, scattered):
        for cond, cp in group.values():
            when(cond, cp.wait_send)
    for cp in (c00, c01, c10, c11):
        cp.wait_send()
    for group in away.values():
        for cond, cp in group:
            when(cond, cp.wait_send)


def local(hamiltonian, h_mask, factor, z_mask, k_mask, block_sizes):
    dma = pltpu.SemaphoreType.DMA
    bf = jnp.bfloat16
    flags = pltpu.SMEM((1, 4), jnp.int32)
    scratch = [
        pltpu.VMEM((512, B), F32), pltpu.VMEM((512, B), F32), flags, flags, flags,
        pltpu.SMEM((32,), jnp.int32), dma((6,)),
        pltpu.VMEM((8, 512, B), F32),
        pltpu.VMEM((8, 512, B), F32),
        pltpu.VMEM((8, 512, B), bf), pltpu.VMEM((8, 512, B), bf),
        pltpu.VMEM((8, 512, B), bf), pltpu.VMEM((8, 512, B), bf),
        pltpu.VMEM((512, B), F32),
        pltpu.VMEM((4, 512, B), F32),
        pltpu.VMEM((CHUNKS, 256, 512), bf), pltpu.VMEM((CHUNKS, 256, 512), bf),
        pltpu.VMEM((2, CHUNKS, 2, 256, 256), F32),
        pltpu.VMEM((2, CHUNKS, 256, 256), F32),
        pltpu.VMEM((2, CHUNKS, 256, 256), F32),
        pltpu.VMEM((2, CHUNKS, 4, 4, HALF, 256), F32),
        pltpu.VMEM((CHUNKS, 2, 2, 256, 256), F32),
        pltpu.VMEM((CHUNKS, 256, 1024), bf), pltpu.VMEM((CHUNKS, 256, 1024), bf),
        pltpu.VMEM((4, CHUNKS, 4, HALF, B), F32),
        pltpu.VMEM((4, CHUNKS, 3, HALF, B), F32),
        pltpu.VMEM((4, B, B), F32), pltpu.VMEM((4, B, B), F32),
        pltpu.VMEM((4, B, B), F32),
        dma((2, 4, 4)), dma((2, 4, 4)), dma((2, 4, 4)), dma((2, 4, 4)),
        dma((2,)), dma((4, 2)), dma((4, 2)),
        dma((2, 2)), dma((2, 2)), dma((2, 2, 4, 4)), dma((2, 2, 4, 4)), dma((2, 2, 4, 4)), dma((2, 2, 4)),
        dma((2, 2, 4)), dma((2, 2, 4)), dma((4, 2, 4)), dma((4, 2, 4)), dma((4,)), dma((4,)), dma((4,)),
    ]
    hbm = pl.BlockSpec(memory_space=pltpu.HBM)
    return pl.pallas_call(
        kernel,
        out_shape=jax.ShapeDtypeStruct((512, B), F32),
        in_specs=[hbm] * 6,
        out_specs=pl.BlockSpec(memory_space=pltpu.VMEM),
        scratch_shapes=scratch,
        compiler_params=pltpu.CompilerParams(
            collective_id=0, has_side_effects=True, vmem_limit_bytes=48 << 20),
        name="congruence",
    )(*[pltpu.with_memory_space_constraint(v, pltpu.HBM) for v in (
        hamiltonian, h_mask.reshape(1, 4), factor, z_mask.reshape(1, 4), k_mask.reshape(1, 4), block_sizes)])


def solution(mesh):
    placed = (
        P("row", "col"),
        P("row", "col"),
        P("row", "col"),
        P("row", "col"),
        P("row", "col"),
        P(),
    )
    return jax.shard_map(
        local, mesh=mesh, in_specs=placed, out_specs=P("row", "col"), check_vma=False
    )
```

```python
import jax
import jax.numpy as jnp
from jax import lax
from jax.experimental import pallas as pl
from jax.experimental.pallas import tpu as pltpu
from jax.sharding import PartitionSpec as P

B = 128
MESH = pl.DeviceIdType.MESH
ORDER = (0, 2, 1, 3)
F32 = jnp.float32
CHUNKS = 2
HALF = B // CHUNKS
OWNER = ((0, 0, 1, 2), (0, 0, 1, 3))


def split(v):
    hi = v.astype(jnp.bfloat16)
    return hi, (v - hi.astype(F32)).astype(jnp.bfloat16)


def when(cond, act):
    if cond is None:
        act()
    else:
        pl.when(cond)(act)


def dot3(ah, al, bh, bl, axis):
    return lax.dot_general(
        jnp.concatenate([ah, ah, al], axis=1), jnp.concatenate([bh, bl, bh], axis=axis),
        (((1,), (axis,)), ((), ())), preferred_element_type=F32)


def kernel(h_hbm, hm_hbm, z_hbm, zm_hbm, km_hbm, size_hbm, out_ref,
           h_ref, z_ref, hm_ref, zm_ref, km_ref, size_ref, in_s,
           hg, zg, ah, al, bh, bl, sw, z1, z1h, z1l, wp, cr, wc, yr, wt, wh, wl, u, xr, fin, fint, tr,
           h_ss, h_rs, z_ss, z_rs, sw_s, z1_ss, z1_rs,
           wc_ss, wc_rs, wy_ss, wy_rs, wa_ss, wa_rs, wf_ss, wf_rs, ux_ss, ux_rs, fd_ss, fm_ss, fd_rs):
    row = lax.axis_index("row")
    col = lax.axis_index("col")
    x, zl = row // 2, row % 2
    y, zh, c = col // 8, (col // 2) % 4, col % 2
    z = zh * 2 + zl

    loads = [
        pltpu.make_async_copy(src, dst, in_s.at[i])
        for i, (src, dst) in enumerate([
            (size_hbm, size_ref), (zm_hbm, zm_ref), (z_hbm, z_ref), (hm_hbm, hm_ref), (h_hbm, h_ref), (km_hbm, km_ref)])
    ]
    for cp in loads:
        cp.start()

    def dev(x_, y_, z_, c_):
        return (x_ * 2 + z_ % 2, (y_ * 4 + z_ // 2) * 2 + c_)

    def remote(src, dst, ss, rs, to):
        return pltpu.make_async_remote_copy(
            src_ref=src, dst_ref=dst, send_sem=ss, recv_sem=rs, device_id=to, device_id_type=MESH)

    sib = dev(x, y, z, 1 - c)
    xpeer = [None] + [dev((x + d) % 4, y, z, c) for d in (1, 2, 3)]
    ypeer = [dev(x, (y + d) % 4, z, c) for d in (1, 2, 3)]
    zpeer = [dev(x, y, (z + 1) % 8, c), dev(x, y, (z + 7) % 8, c)]
    partner = dev(x, y, zh * 2 + c, zl)
    crossed = zl != c
    homed = zl == zh // 2
    diag = x == y

    barrier = pltpu.get_barrier_semaphore()
    for to in [sib] + xpeer[1:] + ypeer + zpeer:
        pl.semaphore_signal(barrier, inc=1, device_id=to, device_id_type=MESH)

    @pl.when(crossed)
    def _():
        pl.semaphore_signal(barrier, inc=1, device_id=partner, device_id_type=MESH)

    lower = x >= y
    for p in range(2):
        @pl.when(x < y)
        def _():
            pl.semaphore_signal(barrier, inc=1, device_id=dev(y, x, 2 * zh + c, p), device_id_type=MESH)

    for b in range(4):
        @pl.when(jnp.logical_and(lower, zl * 4 + b != z))
        def _():
            pl.semaphore_signal(barrier, inc=1, device_id=dev(x, y, zl * 4 + b, c), device_id_type=MESH)

    for q in range(4):
        for p in range(2):
            @pl.when(jnp.logical_not(jnp.logical_and(diag, jnp.logical_and(y == q, c == p))))
            def _():
                pl.semaphore_signal(barrier, inc=1, device_id=dev(y, q, z, p), device_id_type=MESH)

    for cp in loads:
        cp.wait()
    ri = lax.broadcasted_iota(jnp.int32, (B, B), 0)
    ci = lax.broadcasted_iota(jnp.int32, (B, B), 1)
    colok = ci < size_ref[col]
    for s, b in enumerate(ORDER):
        rb = row * 4 + b
        ok = jnp.logical_and(colok, ri < size_ref[rb]).astype(F32)
        up = (ri + rb * B <= ci + col * B).astype(F32)
        zg[z, s * B:(s + 1) * B, :] = z_ref[b * B:(b + 1) * B, :] * (ok * up * zm_ref[0, b].astype(F32))
        hg[z, s * B:(s + 1) * B, :] = h_ref[b * B:(b + 1) * B, :] * (ok * hm_ref[0, b].astype(F32))

    greets = jnp.where(lower, 4 - homed.astype(jnp.int32), 0) + jnp.where(x > y, 2, 0)
    pl.semaphore_wait(barrier, 17 + crossed.astype(jnp.int32) - diag.astype(jnp.int32) + greets)

    swap = remote(zg.at[z], sw, sw_s.at[0], sw_s.at[1], partner)

    @pl.when(crossed)
    def _():
        swap.start()

    @pl.when(jnp.logical_not(crossed))
    def _():
        sw[...] = zg[z]

    def ring(buf, ss, rs):
        made = {}

        def step(st, s):
            for d in range(2):
                if st > 0:
                    made[st - 1, s, d].wait_recv()
                if st == 3 and s % 2 != d:
                    continue
                slot = (z + 8 - st) % 8 if d == 0 else (z + st) % 8
                part = buf.at[slot, pl.ds(s * B, B)]
                cp = remote(part, part, ss.at[d, st, s], rs.at[d, st, s], zpeer[d])
                cp.start()
                made[st, s, d] = cp

        def last(subs):
            for s in subs:
                made[3, s, s % 2].wait_recv()

        def sent():
            for cp in made.values():
                cp.wait_send()

        return step, last, sent

    hstep, hlast, hsent = ring(hg, h_ss, h_rs)
    zstep, zlast, zsent = ring(zg, z_ss, z_rs)

    def parts(buf, hi_ref, lo_ref, dist, rows=slice(0, 512)):
        for slot in {0: [z], 4: [(z + 4) % 8]}.get(dist, [(z + dist) % 8, (z + 8 - dist) % 8]):
            hi, lo = split(buf[slot, rows, :])
            hi_ref[slot, rows, :] = hi
            lo_ref[slot, rows, :] = lo

    pair = (slice(0, 256), slice(256, 512))
    for s in range(4):
        hstep(0, s)
    parts(hg, ah, al, 0)

    @pl.when(crossed)
    def _():
        swap.wait_recv()

    zrow = pl.ds(pl.multiple_of(c * 256, 256), 256)
    sends = []
    for d in (2, 1, 3, 0):
        for p in range(2):
            cp = remote(sw.at[pl.ds(p * 256, 256)], z1.at[y, zrow], z1_ss.at[d, p], z1_rs.at[y, c],
                        dev((x + d) % 4, x, z, p))
            own = jnp.logical_and(diag, c == p) if d == 0 else None
            sends.append((own, cp))
            if own is None:
                cp.start()
            else:
                pl.when(jnp.logical_not(own))(cp.start)

                @pl.when(own)
                def _():
                    z1[y, zrow, :] = sw[p * 256:(p + 1) * 256, :]

    for st in (1, 2, 3):
        for s in range(4):
            hstep(st, s)
        parts(hg, ah, al, st)
    for s in range(4):
        zstep(0, s)
    parts(zg, bh, bl, 0)
    for q in range(4):
        for p in range(2):
            @pl.when(jnp.logical_not(jnp.logical_and(diag, jnp.logical_and(y == q, c == p))))
            def _():
                remote(sw.at[pl.ds(0, 256)], z1.at[q, pl.ds(p * 256, 256)], z1_ss.at[0, 0], z1_rs.at[q, p], sib).wait_recv()

        hi, lo = split(z1[q].T)
        for m in range(CHUNKS):
            z1h[m, q * HALF:(q + 1) * HALF, :] = hi[m * HALF:(m + 1) * HALF, :]
            z1l[m, q * HALF:(q + 1) * HALF, :] = lo[m * HALF:(m + 1) * HALF, :]

    def both(*conds):
        out = conds[0]
        for cond in conds[1:]:
            out = jnp.logical_and(out, cond)
        return out

    kz = [1 - zl, zl]
    uses = [both(x <= y, y <= q) for q in range(4)]

    def first(k, m):
        rh, rl = [jnp.concatenate([ref[2 * q + kz[k]] for q in range(4)], axis=1) for ref in (ah, al)]
        t = dot3(z1h[m], z1l[m], rh, rl, 1)
        wp[k, m, 0] = t[:, :256]
        wp[k, m, 1] = t[:, 256:]
        cp = remote(wp.at[k, m, 1 - c], cr.at[k, m], wc_ss.at[k, m], wc_rs.at[k, m], sib)
        cp.start()
        return cp

    def scatter(k, m, cp):
        cp.wait_recv()
        wc[k, m] = wp[k, m, c] + cr[k, m]
        cps = {}
        for q in (3, 2, 1):
            for src in range(q + 1):
                to = OWNER[m][q]
                if src != to:
                    cond = both(y == src, x <= q)
                    cp = remote(wc.at[k, m, pl.ds(q * HALF, HALF)], yr.at[k, m, q, src],
                                wy_ss.at[k, m, q, src], wy_rs.at[k, m, q, src], dev(x, to, z, c))
                    cps[q, src] = cond, cp
                    when(cond, cp.start)
        return cps

    def spread(k, m, cps):
        out = {}
        for q in (3, 2, 1, 0):
            rows = pl.ds(q * HALF, HALF)
            mine = both(y == OWNER[m][q], x <= q)
            own = wt.at[m, k, c, rows]

            @pl.when(mine)
            def _():
                wt[m, k, c, rows, :] = wc[k, m, rows, :]
                for src in range(q + 1):
                    if src != OWNER[m][q]:
                        cps[q, src][1].wait_recv()
                        wt[m, k, c, rows, :] += yr[k, m, q, src]

            for to in range(q + 1):
                if to != OWNER[m][q]:
                    cond = both(mine, x <= to)
                    out[q, to] = cond, remote(own, own, wa_ss.at[k, m, q, to], wa_rs.at[k, m, q], dev(x, to, z, c))
                    when(cond, out[q, to][1].start)
            out[q, 4] = uses[q], remote(own, own, wf_ss.at[k, m, q], wf_rs.at[k, m, q], sib)
            when(both(mine, uses[q]), out[q, 4][1].start)
        return out

    def forward(k, m, out):
        for q in (3, 2, 1):
            @pl.when(both(uses[q], y != OWNER[m][q]))
            def _():
                out[q, q if q != OWNER[m][q] else 0][1].wait_recv()
                out[q, 4][1].start()

    def gathered(k, m, out):
        for q in range(4):
            when(uses[q], out[q, 4][1].wait_recv)
        for half in range(2):
            hi, lo = split(wt[m, k, half])
            at = (k * 2 + half) * 256
            wh[m, :, at:at + 256] = hi
            wl[m, :, at:at + 256] = lo

    shift = zl * 2 + 3
    near = [zh, (zh + shift) % 4, (zh + 4 - shift % 4) % 4, (zh + 2) % 4]

    def second(js, m):
        rh, rl = [
            jnp.concatenate(
                [jnp.concatenate([ref[2 * near[j] + kz[k], pair[half], :] for k in range(2) for half in range(2)], axis=0)
                 for j in js], axis=1)
            for ref in (bh, bl)]
        t = dot3(wh[m], wl[m], rh, rl, 0)
        for i, j in enumerate(js):
            for q in range(4):
                u[j, m, q] = t[q * HALF:(q + 1) * HALF, i * B:(i + 1) * B]
            for d in (2, 1, 3):
                q = (x + d) % 4
                cond = jnp.logical_and(x <= y, q >= y)
                cp = remote(u.at[j, m, q], xr.at[j, m, d - 1], ux_ss.at[j, m, d], ux_rs.at[j, m, d], xpeer[d])
                scattered[j, m, d] = cond, cp
                when(cond, cp.start)

    scattered = {}
    place = (zh % 2) * 2 + zl
    away = {}

    def deliver(j):
        for m in range(CHUNKS):
            rows = slice(m * HALF, (m + 1) * HALF)
            fin[j, rows, :] = jnp.where(diag, u[j, m, x], 0.0)
            for d in (1, 3, 2):
                @pl.when(jnp.logical_and(lower, (x + 4 - d) % 4 <= y))
                def _():
                    scattered[j, m, d][1].wait_recv()
                    fin[j, rows, :] += xr[j, m, d - 1]

        to = 2 * near[j] + zh // 2
        slot = (near[j] % 2) * 2 + c
        away[j] = [
            (jnp.logical_and(lower, to != z),
             remote(fin.at[j], tr.at[place], fd_ss.at[j], fd_rs.at[place], dev(x, y, to, c))),
            (x > y,
             remote(fint.at[j], tr.at[slot], fm_ss.at[j], fd_rs.at[slot], dev(y, x, 2 * zh + near[j] // 2, zl))),
        ]
        when(away[j][0][0], away[j][0][1].start)

        @pl.when(x > y)
        def _():
            fint[j] = fin[j].T
            away[j][1][1].start()

        @pl.when(jnp.logical_and(lower, to == z))
        def _():
            tr[place] = fin[j]

    c00 = first(0, 0)
    c01 = first(0, 1)
    s00 = scatter(0, 0, c00)
    s01 = scatter(0, 1, c01)
    hlast(range(4))
    parts(hg, ah, al, 4)
    c10 = first(1, 0)
    zstep(1, 0)
    c11 = first(1, 1)
    zstep(1, 1)
    s10 = scatter(1, 0, c10)
    o00 = spread(0, 0, s00)
    s11 = scatter(1, 1, c11)
    o01 = spread(0, 1, s01)
    zstep(1, 2)
    zstep(1, 3)
    parts(zg, bh, bl, 1)
    forward(0, 0, o00)
    o10 = spread(1, 0, s10)
    zstep(2, 0)
    zstep(2, 2)
    forward(0, 1, o01)
    zstep(2, 1)
    o11 = spread(1, 1, s11)
    gathered(0, 0, o00)
    gathered(0, 1, o01)
    forward(1, 0, o10)
    gathered(1, 0, o10)
    zstep(2, 3)
    parts(zg, bh, bl, 2)
    second((0, 1), 0)
    forward(1, 1, o11)
    zstep(3, 0)
    gathered(1, 1, o11)
    second((0, 1), 1)
    zstep(3, 1)
    zstep(3, 2)
    zstep(3, 3)
    parts(zg, bh, bl, 3)
    second((2,), 0)
    second((2,), 1)
    deliver(0)
    deliver(1)
    zlast(range(4))
    parts(zg, bh, bl, 4)
    second((3,), 0)
    second((3,), 1)
    deliver(2)
    deliver(3)
    for b in range(4):
        @pl.when(jnp.logical_not(jnp.logical_and(lower, zl * 4 + b == z)))
        def _():
            remote(fin.at[0], tr.at[b], fd_ss.at[0], fd_rs.at[b], sib).wait_recv()

        out_ref[b * B:(b + 1) * B, :] = tr[b] * km_ref[0, b].astype(F32)

    hsent()
    zsent()

    @pl.when(crossed)
    def _():
        swap.wait_send()

    for own, cp in sends:
        if own is None:
            cp.wait_send()
        else:
            pl.when(jnp.logical_not(own))(cp.wait_send)
    for group in (s00, s01, s10, s11, o00, o01, o10, o11, scattered):
        for cond, cp in group.values():
            when(cond, cp.wait_send)
    for cp in (c00, c01, c10, c11):
        cp.wait_send()
    for group in away.values():
        for cond, cp in group:
            when(cond, cp.wait_send)


def local(hamiltonian, h_mask, factor, z_mask, k_mask, block_sizes):
    dma = pltpu.SemaphoreType.DMA
    bf = jnp.bfloat16
    flags = pltpu.SMEM((1, 4), jnp.int32)
    scratch = [
        pltpu.VMEM((512, B), F32), pltpu.VMEM((512, B), F32), flags, flags, flags,
        pltpu.SMEM((32,), jnp.int32), dma((6,)),
        pltpu.VMEM((8, 512, B), F32),
        pltpu.VMEM((8, 512, B), F32),
        pltpu.VMEM((8, 512, B), bf), pltpu.VMEM((8, 512, B), bf),
        pltpu.VMEM((8, 512, B), bf), pltpu.VMEM((8, 512, B), bf),
        pltpu.VMEM((512, B), F32),
        pltpu.VMEM((4, 512, B), F32),
        pltpu.VMEM((CHUNKS, 256, 512), bf), pltpu.VMEM((CHUNKS, 256, 512), bf),
        pltpu.VMEM((2, CHUNKS, 2, 256, 256), F32),
        pltpu.VMEM((2, CHUNKS, 256, 256), F32),
        pltpu.VMEM((2, CHUNKS, 256, 256), F32),
        pltpu.VMEM((2, CHUNKS, 4, 4, HALF, 256), F32),
        pltpu.VMEM((CHUNKS, 2, 2, 256, 256), F32),
        pltpu.VMEM((CHUNKS, 256, 1024), bf), pltpu.VMEM((CHUNKS, 256, 1024), bf),
        pltpu.VMEM((4, CHUNKS, 4, HALF, B), F32),
        pltpu.VMEM((4, CHUNKS, 3, HALF, B), F32),
        pltpu.VMEM((4, B, B), F32), pltpu.VMEM((4, B, B), F32),
        pltpu.VMEM((4, B, B), F32),
        dma((2, 4, 4)), dma((2, 4, 4)), dma((2, 4, 4)), dma((2, 4, 4)),
        dma((2,)), dma((4, 2)), dma((4, 2)),
        dma((2, 2)), dma((2, 2)), dma((2, 2, 4, 4)), dma((2, 2, 4, 4)), dma((2, 2, 4, 4)), dma((2, 2, 4)),
        dma((2, 2, 4)), dma((2, 2, 4)), dma((4, 2, 4)), dma((4, 2, 4)), dma((4,)), dma((4,)), dma((4,)),
    ]
    hbm = pl.BlockSpec(memory_space=pltpu.HBM)
    return pl.pallas_call(
        kernel,
        out_shape=jax.ShapeDtypeStruct((512, B), F32),
        in_specs=[hbm] * 6,
        out_specs=pl.BlockSpec(memory_space=pltpu.VMEM),
        scratch_shapes=scratch,
        compiler_params=pltpu.CompilerParams(
            collective_id=0, has_side_effects=True, vmem_limit_bytes=48 << 20),
        name="congruence",
    )(*[pltpu.with_memory_space_constraint(v, pltpu.HBM) for v in (
        hamiltonian, h_mask.reshape(1, 4), factor, z_mask.reshape(1, 4), k_mask.reshape(1, 4), block_sizes)])


def solution(mesh):
    placed = (
        P("row", "col"),
        P("row", "col"),
        P("row", "col"),
        P("row", "col"),
        P("row", "col"),
        P(),
    )
    return jax.shard_map(
        local, mesh=mesh, in_specs=placed, out_specs=P("row", "col"), check_vma=False
    )
```

```python
import jax
import jax.numpy as jnp
from jax import lax
from jax.experimental import pallas as pl
from jax.experimental.pallas import tpu as pltpu
from jax.sharding import PartitionSpec as P

B = 128
MESH = pl.DeviceIdType.MESH
ORDER = (0, 2, 1, 3)
F32 = jnp.float32
CHUNKS = 2
HALF = B // CHUNKS
OWNER = ((0, 0, 1, 2), (0, 0, 1, 3))


def split(v):
    hi = v.astype(jnp.bfloat16)
    return hi, (v - hi.astype(F32)).astype(jnp.bfloat16)


def when(cond, act):
    if cond is None:
        act()
    else:
        pl.when(cond)(act)


def dot3(ah, al, bh, bl, axis):
    return lax.dot_general(
        jnp.concatenate([ah, ah, al], axis=1), jnp.concatenate([bh, bl, bh], axis=axis),
        (((1,), (axis,)), ((), ())), preferred_element_type=F32)


def kernel(h_hbm, hm_hbm, z_hbm, zm_hbm, km_hbm, size_hbm, out_ref,
           h_ref, z_ref, hm_ref, zm_ref, km_ref, size_ref, in_s,
           hg, zg, ah, al, bh, bl, sw, z1, z1h, z1l, wp, cr, wc, yr, wt, wh, wl, u, xr, fin, fint, tr,
           h_ss, h_rs, z_ss, z_rs, sw_s, z1_ss, z1_rs,
           wc_ss, wc_rs, wy_ss, wy_rs, wa_ss, wa_rs, wf_ss, wf_rs, ux_ss, ux_rs, fd_ss, fm_ss, fd_rs):
    row = lax.axis_index("row")
    col = lax.axis_index("col")
    x, zl = row // 2, row % 2
    y, zh, c = col // 8, (col // 2) % 4, col % 2
    z = zh * 2 + zl

    loads = [
        pltpu.make_async_copy(src, dst, in_s.at[i])
        for i, (src, dst) in enumerate([
            (size_hbm, size_ref), (zm_hbm, zm_ref), (z_hbm, z_ref), (hm_hbm, hm_ref), (h_hbm, h_ref), (km_hbm, km_ref)])
    ]
    for cp in loads:
        cp.start()

    def dev(x_, y_, z_, c_):
        return (x_ * 2 + z_ % 2, (y_ * 4 + z_ // 2) * 2 + c_)

    def remote(src, dst, ss, rs, to):
        return pltpu.make_async_remote_copy(
            src_ref=src, dst_ref=dst, send_sem=ss, recv_sem=rs, device_id=to, device_id_type=MESH)

    sib = dev(x, y, z, 1 - c)
    xpeer = [None] + [dev((x + d) % 4, y, z, c) for d in (1, 2, 3)]
    ypeer = [dev(x, (y + d) % 4, z, c) for d in (1, 2, 3)]
    zpeer = [dev(x, y, (z + 1) % 8, c), dev(x, y, (z + 7) % 8, c)]
    partner = dev(x, y, zh * 2 + c, zl)
    crossed = zl != c
    homed = zl == zh // 2
    diag = x == y

    barrier = pltpu.get_barrier_semaphore()
    for to in [sib] + xpeer[1:] + ypeer + zpeer:
        pl.semaphore_signal(barrier, inc=1, device_id=to, device_id_type=MESH)

    @pl.when(crossed)
    def _():
        pl.semaphore_signal(barrier, inc=1, device_id=partner, device_id_type=MESH)

    lower = x >= y
    for p in range(2):
        @pl.when(x < y)
        def _():
            pl.semaphore_signal(barrier, inc=1, device_id=dev(y, x, 2 * zh + c, p), device_id_type=MESH)

    for b in range(4):
        @pl.when(jnp.logical_and(lower, zl * 4 + b != z))
        def _():
            pl.semaphore_signal(barrier, inc=1, device_id=dev(x, y, zl * 4 + b, c), device_id_type=MESH)

    for q in range(4):
        for p in range(2):
            @pl.when(jnp.logical_not(jnp.logical_and(diag, jnp.logical_and(y == q, c == p))))
            def _():
                pl.semaphore_signal(barrier, inc=1, device_id=dev(y, q, z, p), device_id_type=MESH)

    for cp in loads[:3]:
        cp.wait()
    ri = lax.broadcasted_iota(jnp.int32, (B, B), 0)
    ci = lax.broadcasted_iota(jnp.int32, (B, B), 1)
    colok = ci < size_ref[col]
    for s, b in enumerate(ORDER):
        rb = row * 4 + b
        ok = jnp.logical_and(colok, ri < size_ref[rb]).astype(F32)
        up = (ri + rb * B <= ci + col * B).astype(F32)
        zg[z, s * B:(s + 1) * B, :] = z_ref[b * B:(b + 1) * B, :] * (ok * up * zm_ref[0, b].astype(F32))
    for cp in loads[3:5]:
        cp.wait()
    for s, b in enumerate(ORDER):
        ok = jnp.logical_and(colok, ri < size_ref[row * 4 + b]).astype(F32)
        hg[z, s * B:(s + 1) * B, :] = h_ref[b * B:(b + 1) * B, :] * (ok * hm_ref[0, b].astype(F32))

    greets = jnp.where(lower, 4 - homed.astype(jnp.int32), 0) + jnp.where(x > y, 2, 0)
    pl.semaphore_wait(barrier, 17 + crossed.astype(jnp.int32) - diag.astype(jnp.int32) + greets)

    swap = remote(zg.at[z], sw, sw_s.at[0], sw_s.at[1], partner)

    @pl.when(crossed)
    def _():
        swap.start()

    @pl.when(jnp.logical_not(crossed))
    def _():
        sw[...] = zg[z]

    def ring(buf, ss, rs):
        made = {}

        def step(st, s):
            for d in range(2):
                if st > 0:
                    made[st - 1, s, d].wait_recv()
                if st == 3 and s % 2 != d:
                    continue
                slot = (z + 8 - st) % 8 if d == 0 else (z + st) % 8
                part = buf.at[slot, pl.ds(s * B, B)]
                cp = remote(part, part, ss.at[d, st, s], rs.at[d, st, s], zpeer[d])
                cp.start()
                made[st, s, d] = cp

        def last(subs):
            for s in subs:
                made[3, s, s % 2].wait_recv()

        def sent():
            for cp in made.values():
                cp.wait_send()

        return step, last, sent

    hstep, hlast, hsent = ring(hg, h_ss, h_rs)
    zstep, zlast, zsent = ring(zg, z_ss, z_rs)

    def parts(buf, hi_ref, lo_ref, dist, rows=slice(0, 512)):
        for slot in {0: [z], 4: [(z + 4) % 8]}.get(dist, [(z + dist) % 8, (z + 8 - dist) % 8]):
            hi, lo = split(buf[slot, rows, :])
            hi_ref[slot, rows, :] = hi
            lo_ref[slot, rows, :] = lo

    pair = (slice(0, 256), slice(256, 512))
    for s in range(4):
        hstep(0, s)
    parts(hg, ah, al, 0)

    @pl.when(crossed)
    def _():
        swap.wait_recv()

    zrow = pl.ds(pl.multiple_of(c * 256, 256), 256)
    sends = []
    for d in (2, 1, 3, 0):
        for p in range(2):
            cp = remote(sw.at[pl.ds(p * 256, 256)], z1.at[y, zrow], z1_ss.at[d, p], z1_rs.at[y, c],
                        dev((x + d) % 4, x, z, p))
            own = jnp.logical_and(diag, c == p) if d == 0 else None
            sends.append((own, cp))
            if own is None:
                cp.start()
            else:
                pl.when(jnp.logical_not(own))(cp.start)

                @pl.when(own)
                def _():
                    z1[y, zrow, :] = sw[p * 256:(p + 1) * 256, :]

    for st in (1, 2, 3):
        for s in range(4):
            hstep(st, s)
        parts(hg, ah, al, st)
    for s in range(4):
        zstep(0, s)
    parts(zg, bh, bl, 0)
    for q in range(4):
        for p in range(2):
            @pl.when(jnp.logical_not(jnp.logical_and(diag, jnp.logical_and(y == q, c == p))))
            def _():
                remote(sw.at[pl.ds(0, 256)], z1.at[q, pl.ds(p * 256, 256)], z1_ss.at[0, 0], z1_rs.at[q, p], sib).wait_recv()

        hi, lo = split(z1[q].T)
        for m in range(CHUNKS):
            z1h[m, q * HALF:(q + 1) * HALF, :] = hi[m * HALF:(m + 1) * HALF, :]
            z1l[m, q * HALF:(q + 1) * HALF, :] = lo[m * HALF:(m + 1) * HALF, :]

    def both(*conds):
        out = conds[0]
        for cond in conds[1:]:
            out = jnp.logical_and(out, cond)
        return out

    kz = [1 - zl, zl]
    uses = [both(x <= y, y <= q) for q in range(4)]

    def first(k, m):
        rh, rl = [jnp.concatenate([ref[2 * q + kz[k]] for q in range(4)], axis=1) for ref in (ah, al)]
        t = dot3(z1h[m], z1l[m], rh, rl, 1)
        wp[k, m, 0] = t[:, :256]
        wp[k, m, 1] = t[:, 256:]
        cp = remote(wp.at[k, m, 1 - c], cr.at[k, m], wc_ss.at[k, m], wc_rs.at[k, m], sib)
        cp.start()
        return cp

    def scatter(k, m, cp):
        cp.wait_recv()
        wc[k, m] = wp[k, m, c] + cr[k, m]
        cps = {}
        for q in (3, 2, 1):
            for src in range(q + 1):
                to = OWNER[m][q]
                if src != to:
                    cond = both(y == src, x <= q)
                    cp = remote(wc.at[k, m, pl.ds(q * HALF, HALF)], yr.at[k, m, q, src],
                                wy_ss.at[k, m, q, src], wy_rs.at[k, m, q, src], dev(x, to, z, c))
                    cps[q, src] = cond, cp
                    when(cond, cp.start)
        return cps

    def spread(k, m, cps):
        out = {}
        for q in (3, 2, 1, 0):
            rows = pl.ds(q * HALF, HALF)
            mine = both(y == OWNER[m][q], x <= q)
            own = wt.at[m, k, c, rows]

            @pl.when(mine)
            def _():
                wt[m, k, c, rows, :] = wc[k, m, rows, :]
                for src in range(q + 1):
                    if src != OWNER[m][q]:
                        cps[q, src][1].wait_recv()
                        wt[m, k, c, rows, :] += yr[k, m, q, src]

            for to in range(q + 1):
                if to != OWNER[m][q]:
                    cond = both(mine, x <= to)
                    out[q, to] = cond, remote(own, own, wa_ss.at[k, m, q, to], wa_rs.at[k, m, q], dev(x, to, z, c))
                    when(cond, out[q, to][1].start)
            out[q, 4] = uses[q], remote(own, own, wf_ss.at[k, m, q], wf_rs.at[k, m, q], sib)
            when(both(mine, uses[q]), out[q, 4][1].start)
        return out

    def forward(k, m, out):
        for q in (3, 2, 1):
            @pl.when(both(uses[q], y != OWNER[m][q]))
            def _():
                out[q, q if q != OWNER[m][q] else 0][1].wait_recv()
                out[q, 4][1].start()

    def gathered(k, m, out):
        for q in range(4):
            when(uses[q], out[q, 4][1].wait_recv)
        for half in range(2):
            hi, lo = split(wt[m, k, half])
            at = (k * 2 + half) * 256
            wh[m, :, at:at + 256] = hi
            wl[m, :, at:at + 256] = lo

    shift = zl * 2 + 3
    near = [zh, (zh + shift) % 4, (zh + 4 - shift % 4) % 4, (zh + 2) % 4]

    def second(js, m):
        rh, rl = [
            jnp.concatenate(
                [jnp.concatenate([ref[2 * near[j] + kz[k], pair[half], :] for k in range(2) for half in range(2)], axis=0)
                 for j in js], axis=1)
            for ref in (bh, bl)]
        t = dot3(wh[m], wl[m], rh, rl, 0)
        for i, j in enumerate(js):
            for q in range(4):
                u[j, m, q] = t[q * HALF:(q + 1) * HALF, i * B:(i + 1) * B]
            for d in (2, 1, 3):
                q = (x + d) % 4
                cond = jnp.logical_and(x <= y, q >= y)
                cp = remote(u.at[j, m, q], xr.at[j, m, d - 1], ux_ss.at[j, m, d], ux_rs.at[j, m, d], xpeer[d])
                scattered[j, m, d] = cond, cp
                when(cond, cp.start)

    scattered = {}
    place = (zh % 2) * 2 + zl
    away = {}

    def deliver(j):
        for m in range(CHUNKS):
            rows = slice(m * HALF, (m + 1) * HALF)
            fin[j, rows, :] = jnp.where(diag, u[j, m, x], 0.0)
            for d in (1, 3, 2):
                @pl.when(jnp.logical_and(lower, (x + 4 - d) % 4 <= y))
                def _():
                    scattered[j, m, d][1].wait_recv()
                    fin[j, rows, :] += xr[j, m, d - 1]

        to = 2 * near[j] + zh // 2
        slot = (near[j] % 2) * 2 + c
        away[j] = [
            (jnp.logical_and(lower, to != z),
             remote(fin.at[j], tr.at[place], fd_ss.at[j], fd_rs.at[place], dev(x, y, to, c))),
            (x > y,
             remote(fint.at[j], tr.at[slot], fm_ss.at[j], fd_rs.at[slot], dev(y, x, 2 * zh + near[j] // 2, zl))),
        ]
        when(away[j][0][0], away[j][0][1].start)

        @pl.when(x > y)
        def _():
            fint[j] = fin[j].T
            away[j][1][1].start()

        @pl.when(jnp.logical_and(lower, to == z))
        def _():
            tr[place] = fin[j]

    c00 = first(0, 0)
    c01 = first(0, 1)
    s00 = scatter(0, 0, c00)
    s01 = scatter(0, 1, c01)
    hlast(range(4))
    parts(hg, ah, al, 4)
    c10 = first(1, 0)
    zstep(1, 0)
    c11 = first(1, 1)
    zstep(1, 1)
    s10 = scatter(1, 0, c10)
    o00 = spread(0, 0, s00)
    s11 = scatter(1, 1, c11)
    o01 = spread(0, 1, s01)
    zstep(1, 2)
    zstep(1, 3)
    parts(zg, bh, bl, 1)
    forward(0, 0, o00)
    o10 = spread(1, 0, s10)
    zstep(2, 0)
    zstep(2, 2)
    forward(0, 1, o01)
    zstep(2, 1)
    o11 = spread(1, 1, s11)
    gathered(0, 0, o00)
    gathered(0, 1, o01)
    forward(1, 0, o10)
    gathered(1, 0, o10)
    zstep(2, 3)
    parts(zg, bh, bl, 2)
    second((0, 1), 0)
    forward(1, 1, o11)
    zstep(3, 0)
    gathered(1, 1, o11)
    second((0, 1), 1)
    zstep(3, 1)
    zstep(3, 2)
    zstep(3, 3)
    parts(zg, bh, bl, 3)
    second((2,), 0)
    second((2,), 1)
    deliver(0)
    deliver(1)
    zlast(range(4))
    parts(zg, bh, bl, 4)
    second((3,), 0)
    second((3,), 1)
    deliver(2)
    deliver(3)
    loads[5].wait()
    for b in range(4):
        @pl.when(jnp.logical_not(jnp.logical_and(lower, zl * 4 + b == z)))
        def _():
            remote(fin.at[0], tr.at[b], fd_ss.at[0], fd_rs.at[b], sib).wait_recv()

        out_ref[b * B:(b + 1) * B, :] = tr[b] * km_ref[0, b].astype(F32)

    hsent()
    zsent()

    @pl.when(crossed)
    def _():
        swap.wait_send()

    for own, cp in sends:
        if own is None:
            cp.wait_send()
        else:
            pl.when(jnp.logical_not(own))(cp.wait_send)
    for group in (s00, s01, s10, s11, o00, o01, o10, o11, scattered):
        for cond, cp in group.values():
            when(cond, cp.wait_send)
    for cp in (c00, c01, c10, c11):
        cp.wait_send()
    for group in away.values():
        for cond, cp in group:
            when(cond, cp.wait_send)


def local(hamiltonian, h_mask, factor, z_mask, k_mask, block_sizes):
    dma = pltpu.SemaphoreType.DMA
    bf = jnp.bfloat16
    flags = pltpu.SMEM((1, 4), jnp.int32)
    scratch = [
        pltpu.VMEM((512, B), F32), pltpu.VMEM((512, B), F32), flags, flags, flags,
        pltpu.SMEM((32,), jnp.int32), dma((6,)),
        pltpu.VMEM((8, 512, B), F32),
        pltpu.VMEM((8, 512, B), F32),
        pltpu.VMEM((8, 512, B), bf), pltpu.VMEM((8, 512, B), bf),
        pltpu.VMEM((8, 512, B), bf), pltpu.VMEM((8, 512, B), bf),
        pltpu.VMEM((512, B), F32),
        pltpu.VMEM((4, 512, B), F32),
        pltpu.VMEM((CHUNKS, 256, 512), bf), pltpu.VMEM((CHUNKS, 256, 512), bf),
        pltpu.VMEM((2, CHUNKS, 2, 256, 256), F32),
        pltpu.VMEM((2, CHUNKS, 256, 256), F32),
        pltpu.VMEM((2, CHUNKS, 256, 256), F32),
        pltpu.VMEM((2, CHUNKS, 4, 4, HALF, 256), F32),
        pltpu.VMEM((CHUNKS, 2, 2, 256, 256), F32),
        pltpu.VMEM((CHUNKS, 256, 1024), bf), pltpu.VMEM((CHUNKS, 256, 1024), bf),
        pltpu.VMEM((4, CHUNKS, 4, HALF, B), F32),
        pltpu.VMEM((4, CHUNKS, 3, HALF, B), F32),
        pltpu.VMEM((4, B, B), F32), pltpu.VMEM((4, B, B), F32),
        pltpu.VMEM((4, B, B), F32),
        dma((2, 4, 4)), dma((2, 4, 4)), dma((2, 4, 4)), dma((2, 4, 4)),
        dma((2,)), dma((4, 2)), dma((4, 2)),
        dma((2, 2)), dma((2, 2)), dma((2, 2, 4, 4)), dma((2, 2, 4, 4)), dma((2, 2, 4, 4)), dma((2, 2, 4)),
        dma((2, 2, 4)), dma((2, 2, 4)), dma((4, 2, 4)), dma((4, 2, 4)), dma((4,)), dma((4,)), dma((4,)),
    ]
    hbm = pl.BlockSpec(memory_space=pltpu.HBM)
    return pl.pallas_call(
        kernel,
        out_shape=jax.ShapeDtypeStruct((512, B), F32),
        in_specs=[hbm] * 6,
        out_specs=pl.BlockSpec(memory_space=pltpu.VMEM),
        scratch_shapes=scratch,
        compiler_params=pltpu.CompilerParams(
            collective_id=0, has_side_effects=True, vmem_limit_bytes=48 << 20),
        name="congruence",
    )(*[pltpu.with_memory_space_constraint(v, pltpu.HBM) for v in (
        hamiltonian, h_mask.reshape(1, 4), factor, z_mask.reshape(1, 4), k_mask.reshape(1, 4), block_sizes)])


def solution(mesh):
    placed = (
        P("row", "col"),
        P("row", "col"),
        P("row", "col"),
        P("row", "col"),
        P("row", "col"),
        P(),
    )
    return jax.shard_map(
        local, mesh=mesh, in_specs=placed, out_specs=P("row", "col"), check_vma=False
    )
```
